32 devices in a mesh: dp: 2 (over x), row: 4 (over z), col: 4 (over y, core).
Axes of the slice: x: 2, y: 2, z: 4, core: 2. Of those that a mesh axis runs over, the one named last changes fastest.
Arguments:
- block_input: bfloat16 [1024, 1024], P(('dp', 'col'), 'row'), may hold values from -6 to 6
- attn_gain: float32 [1024], P('row'), may hold values from 0.5 to 1.5
- query_weight: bfloat16 [1024, 1024], P('row', 'col'), may hold values from -0.1875 to 0.1875
- key_weight: bfloat16 [1024, 1024], P('row', 'col'), may hold values from -0.1875 to 0.1875
- value_weight: bfloat16 [1024, 2048], P('row', 'col'), may hold values from -0.1875 to 0.1875
- gate_weight: bfloat16 [1024, 2048], P('row', 'col'), may hold values from -0.1875 to 0.1875
- decay_weight: bfloat16 [1024, 8], P('row', 'col'), may hold values from -0.1875 to 0.1875
- beta_weight: bfloat16 [1024, 8], P('row', 'col'), may hold values from -0.1875 to 0.1875
- query_conv: float32 [4, 1024], P(None, 'col'), may hold values from -3 to 3
- key_conv: float32 [4, 1024], P(None, 'col'), may hold values from -3 to 3
- value_conv: float32 [4, 2048], P(None, 'col'), may hold values from -3 to 3
- decay_log: float32 [8], P('col'), may hold values from -4 to 0.5
- decay_bias: float32 [8], P('col'), may hold values from -3 to 0
- head_gain: float32 [256], replicated, may hold values from 0.5 to 1.5
- out_weight: bfloat16 [2048, 1024], P('col', 'row'), may hold values from -0.1875 to 0.1875
- ffn_gain: float32 [1024], P('row'), may hold values from 0.5 to 1.5
- ffn_gate: bfloat16 [1024, 2816], P('row', 'col'), may hold values from -0.1875 to 0.1875
- ffn_up: bfloat16 [1024, 2816], P('row', 'col'), may hold values from -0.1875 to 0.1875
- ffn_down: bfloat16 [2816, 1024], P('col', 'row'), may hold values from -0.15625 to 0.15625
- out_grad: bfloat16 [1024, 1024], P(('dp', 'col'), 'row'), may hold values from -6 to 6
- seq_starts: int32 [8, 1], replicated, may hold values from 0 to 64, as said below
- seq_lengths: int32 [8, 1], replicated, may hold values from 1 to 128, as said below
Outputs:
- output: bfloat16 [1024, 1024], P(('dp', 'col'), 'row')
- input_grad: float32 [1024, 1024], P(('dp', 'col'), 'row')
- attn_gain_grad: float32 [1024], P('row')
- query_weight_grad: float32 [1024, 1024], P('row', 'col')
- key_weight_grad: float32 [1024, 1024], P('row', 'col')
- value_weight_grad: float32 [1024, 2048], P('row', 'col')
- gate_weight_grad: float32 [1024, 2048], P('row', 'col')
- decay_weight_grad: float32 [1024, 8], P('row', 'col')
- beta_weight_grad: float32 [1024, 8], P('row', 'col')
- query_conv_grad: float32 [4, 1024], P(None, 'col')
- key_conv_grad: float32 [4, 1024], P(None, 'col')
- value_conv_grad: float32 [4, 2048], P(None, 'col')
- decay_log_grad: float32 [8], P('col')
- decay_bias_grad: float32 [8], P('col')
- head_gain_grad: float32 [256], replicated
- out_weight_grad: float32 [2048, 1024], P('col', 'row')
- ffn_gain_grad: float32 [1024], P('row')
- ffn_gate_grad: float32 [1024, 2816], P('row', 'col')
- ffn_up_grad: float32 [1024, 2816], P('row', 'col')
- ffn_down_grad: float32 [2816, 1024], P('col', 'row')
The draws below stay inside these ranges and needn't reach their ends.
Inputs may be any that keep to these rules, and one draw needn't show every extreme that they name: `seq_starts`: sequences of a slot are in order and do not intersect; sequence i starts within tokens i * 128 to i * 128 + 128 // 2 of its slot and ends by (i + 1) * 128 - 1; in every draw some sequence starts at the last of these in the slot's last region. `seq_lengths`: in every draw some sequence is 128 tokens long.
All inputs are finite; a program needn't handle non-finite values.
Results may differ from the reference program's by a relative error of at most 0.012.
Values may be sent and summed in bfloat16 or wider, within the bound.
A program may use at most 128 MiB of HBM per device.

```python
import jax
import jax.numpy as jnp
from jax import lax

D = 1024
HEADS = 8
DV = 256
FF = 2816
KCONV = 4
BLOCK = 64
NSEQ = 1
SLOT = 128
SLOTS = 8
TOKENS = 1024
KEYS = 1024
VALS = 2048


def sequence_layout(key):
    region = SLOT // NSEQ
    base = jax.random.fold_in(key, 7)
    key_cap = jax.random.fold_in(base, 1)
    key_len = jax.random.fold_in(base, 2)
    key_off = jax.random.fold_in(base, 3)
    key_pick = jax.random.fold_in(base, 4)
    key_late = jax.random.fold_in(base, 5)
    divisor = 1 + jax.random.randint(key_cap, (SLOTS, 1), 0, 2)
    capacity = region // divisor
    raw_len = jax.random.randint(key_len, (SLOTS, NSEQ), 0, 1 << 20)
    lengths = raw_len % (capacity - capacity // 2 + 1) + capacity // 2
    lengths = jnp.maximum(lengths, 1)
    picked = jax.random.randint(key_pick, (), 0, SLOTS * NSEQ)
    flat_index = jnp.arange(SLOTS * NSEQ, dtype=jnp.int32).reshape(SLOTS, NSEQ)
    late_slot = jax.random.randint(key_late, (), 0, SLOTS)
    late_flat = late_slot * NSEQ + NSEQ - 1
    late_slot = jnp.where(late_flat == picked, (late_slot + 1) % SLOTS, late_slot)
    late_flat = late_slot * NSEQ + NSEQ - 1
    lengths = jnp.where(flat_index == picked, region, lengths)
    lengths = jnp.where(flat_index == late_flat, region // 2, lengths).astype(jnp.int32)
    raw_off = jax.random.randint(key_off, (SLOTS, NSEQ), 0, 1 << 20)
    room = jnp.minimum(region - lengths, region // 2)
    offsets = raw_off % (room + 1)
    offsets = jnp.where(flat_index == late_flat, region // 2, offsets)
    starts = offsets + jnp.arange(NSEQ, dtype=jnp.int32)[None, :] * region
    return (starts.astype(jnp.int32), lengths)


def draw_seq_starts(key, part):
    return sequence_layout(key)[0]


def draw_seq_lengths(key, part):
    return sequence_layout(key)[1]


def shard_levels(stream_key, shape, cuts, smallest, largest):
    level, own = 1.0, jax.random.fold_in(stream_key, 6)
    for dim, blocks in cuts:
        heights = jnp.exp(jax.random.uniform(jax.random.fold_in(own, dim), (blocks,), jnp.float32, smallest / len(cuts), largest / len(cuts)))
        level = level * jnp.repeat(heights, shape[dim] // blocks).reshape([-1 if axis == dim else 1 for axis in range(len(shape))])
    return level


def centred(rng, dims, deviation, reach, split=(), kind=jnp.bfloat16):
    entries = jax.random.normal(rng, dims, jnp.float32) * deviation
    if len(split) > 0:
        entries = shard_levels(rng, dims, split, -0.22, 0.18) * entries
    return jnp.clip(entries, min=-reach, max=reach).astype(kind)


def setup_inputs(seed: int = 0) -> dict:
    arg_keys = jax.random.split(jax.random.key(seed), 23)
    block_input = centred(arg_keys[0], (TOKENS, D), 1.0, 6.0, ((0, 8), (1, 4)))
    attn_gain = jnp.clip(1.0 + 0.1 * jax.random.normal(arg_keys[1], (D,), jnp.float32), 0.5, 1.5)
    query_weight = centred(arg_keys[2], (D, KEYS), D ** -0.5, 0.1875, ((0, 4), (1, 4)))
    key_weight = centred(arg_keys[3], (D, KEYS), D ** -0.5, 0.1875, ((0, 4), (1, 4)))
    value_weight = centred(arg_keys[4], (D, VALS), D ** -0.5, 0.1875, ((0, 4), (1, 4)))
    gate_weight = centred(arg_keys[5], (D, VALS), D ** -0.5, 0.1875, ((0, 4), (1, 4)))
    decay_weight = centred(arg_keys[6], (D, HEADS), D ** -0.5, 0.1875, ((0, 4), (1, 4)))
    beta_weight = centred(arg_keys[7], (D, HEADS), D ** -0.5, 0.1875, ((0, 4), (1, 4)))
    query_conv = centred(arg_keys[8], (KCONV, KEYS), 0.5, 3.0, ((1, 4),), jnp.float32)
    key_conv = centred(arg_keys[9], (KCONV, KEYS), 0.5, 3.0, ((1, 4),), jnp.float32)
    value_conv = centred(arg_keys[10], (KCONV, VALS), 0.5, 3.0, ((1, 4),), jnp.float32)
    decay_log = jnp.clip(-4.0 + 4.5 * jax.random.uniform(arg_keys[11], (HEADS,), jnp.float32) ** shard_levels(arg_keys[11], (HEADS,), ((0, 4),), -0.2, 0.2), -4.0, 0.5)
    decay_bias = jnp.clip(-3.0 + 3.0 * jax.random.uniform(arg_keys[12], (HEADS,), jnp.float32) ** shard_levels(arg_keys[12], (HEADS,), ((0, 4),), -0.2, 0.2), -3.0, 0.0)
    head_gain = jnp.clip(1.0 + 0.1 * jax.random.normal(arg_keys[13], (DV,), jnp.float32), 0.5, 1.5)
    out_weight = centred(arg_keys[14], (VALS, D), D ** -0.5, 0.1875, ((0, 4), (1, 4)))
    ffn_gain = jnp.clip(1.0 + 0.1 * jax.random.normal(arg_keys[15], (D,), jnp.float32), 0.5, 1.5)
    ffn_gate = centred(arg_keys[16], (D, FF), D ** -0.5, 0.1875, ((0, 4), (1, 4)))
    ffn_up = centred(arg_keys[17], (D, FF), D ** -0.5, 0.1875, ((0, 4), (1, 4)))
    ffn_down = centred(arg_keys[18], (FF, D), (FF // 2) ** -0.5, 0.15625, ((0, 4), (1, 4)))
    out_grad = centred(arg_keys[19], (TOKENS, D), 1.0, 6.0, ((0, 8), (1, 4)))
    seq_starts = draw_seq_starts(jax.random.fold_in(arg_keys[22], 71), 0)
    seq_lengths = draw_seq_lengths(jax.random.fold_in(arg_keys[22], 71), 0)
    return dict(block_input=block_input, attn_gain=attn_gain, query_weight=query_weight, key_weight=key_weight, value_weight=value_weight, gate_weight=gate_weight, decay_weight=decay_weight, beta_weight=beta_weight, query_conv=query_conv, key_conv=key_conv, value_conv=value_conv, decay_log=decay_log, decay_bias=decay_bias, head_gain=head_gain, out_weight=out_weight, ffn_gain=ffn_gain, ffn_gate=ffn_gate, ffn_up=ffn_up, ffn_down=ffn_down, out_grad=out_grad, seq_starts=seq_starts, seq_lengths=seq_lengths)


epsilon = 1e-06
highest = lax.Precision.HIGHEST

def segment_info(starts, lengths, count):
    position = jnp.arange(count, dtype=jnp.int32)[:, None]
    begun = (position >= starts[None, :]).astype(jnp.int32)
    ended = (position >= (starts + lengths)[None, :]).astype(jnp.int32)
    segment = lax.optimization_barrier(jnp.sum(begun + ended, axis=1)).astype(jnp.int32)
    inside = lax.optimization_barrier(jnp.sum(begun - ended, axis=1)).astype(jnp.float32)
    return (segment, inside)

def short_conv(signal, kernel, segment):
    length = signal.shape[0]
    tap_count = kernel.shape[0]
    running_total = kernel[tap_count - 1] * signal
    for offset in range(1, tap_count):
        moved = jnp.pad(signal, ((offset, 0), (0, 0)))[:length]
        earlier = jnp.pad(segment, (offset, 0), constant_values=-1)[:length]
        running_total = running_total + kernel[tap_count - 1 - offset] * jnp.where((earlier == segment)[:, None], moved, 0.0)
    return jax.nn.silu(running_total)

def unit_heads(signal, head_count):
    shaped = signal.reshape(signal.shape[0], head_count, -1)
    return shaped * lax.rsqrt(lax.optimization_barrier(jnp.sum(shaped * shaped, axis=-1, keepdims=True)) + epsilon)

def delta_rule(queries, key_heads, value_heads, write_rate, log_decay, segment):
    length, head_count, key_size = queries.shape
    value_size = value_heads.shape[2]
    blocks = length // BLOCK
    position = jnp.arange(BLOCK, dtype=jnp.int32)
    later_mask = position[:, None] > position[None, :]
    upto_mask = position[:, None] >= position[None, :]

    def advance(carry, pieces):
        memory, last_segment = carry
        block_query, block_key, block_value, block_rate, block_decay, block_segment = pieces
        cumulative = jnp.cumsum(block_decay, axis=0)
        same_segment = block_segment[:, None] == block_segment[None, :]
        strict = (same_segment & later_mask).astype(jnp.float32)
        within = (same_segment & upto_mask).astype(jnp.float32)
        carried = (block_segment == last_segment).astype(jnp.float32)
        decay_ratio = jnp.exp(jnp.minimum(cumulative.T[:, :, None] - cumulative.T[:, None, :], 0.0))
        key_dots = jnp.einsum('thd,jhd->htj', block_key, block_key, precision=highest)
        query_dots = jnp.einsum('thd,jhd->htj', block_query, block_key, precision=highest)
        lower_part = block_rate.T[:, :, None] * decay_ratio * key_dots * strict
        decayed = (jnp.exp(cumulative) * carried[:, None]).T
        recalled = jnp.einsum('hvk,thk->htv', memory, block_key, precision=highest)
        target = block_rate.T[:, :, None] * (jnp.transpose(block_value, (1, 0, 2)) - decayed[:, :, None] * recalled)
        writes = jax.scipy.linalg.solve_triangular(lower_part, target, lower=True, unit_diagonal=True)
        readout = decayed[:, :, None] * jnp.einsum('hvk,thk->htv', memory, block_query, precision=highest)
        readout = readout + jnp.einsum('htj,hjv->htv', decay_ratio * query_dots * within, writes, precision=highest)
        closing = (block_segment == block_segment[-1]).astype(jnp.float32)
        ending = jnp.exp(cumulative[-1][None, :] - cumulative) * closing[:, None]
        memory = memory * decayed[:, -1][:, None, None] + jnp.einsum('jh,hjv,jhk->hvk', ending, writes, block_key, precision=highest)
        return ((memory, block_segment[-1]), jnp.transpose(readout, (1, 0, 2)))

    def blocked(array):
        return array.reshape((blocks, BLOCK) + array.shape[1:])
    initial = (jnp.zeros((head_count, value_size, key_size), jnp.float32), jnp.array(-1, jnp.int32))
    final_carry, stacked = lax.scan(advance, initial, (blocked(queries), blocked(key_heads), blocked(value_heads), blocked(write_rate), blocked(log_decay), blocked(segment)))
    return stacked.reshape(length, head_count, value_size)

def token_mixer(linears, params, segment, inside):
    query_lin, key_lin, value_lin, gate_lin, decay_lin, rate_lin = linears
    conv_query, conv_key, conv_value, log_rate, rate_bias, norm_gain = params
    head_count = log_rate.shape[0]
    length = query_lin.shape[0]
    queries = unit_heads(short_conv(query_lin, conv_query, segment), head_count)
    queries = queries * queries.shape[-1] ** (-0.5)
    key_heads = unit_heads(short_conv(key_lin, conv_key, segment), head_count)
    value_heads = short_conv(value_lin, conv_value, segment).reshape(length, head_count, -1)
    write_rate = jax.nn.sigmoid(rate_lin)
    log_decay = -jnp.exp(log_rate) * jax.nn.softplus(decay_lin + rate_bias)
    mixed_heads = delta_rule(queries, key_heads, value_heads, write_rate, log_decay, segment)
    normed = mixed_heads * lax.rsqrt(lax.optimization_barrier(jnp.mean(mixed_heads * mixed_heads, axis=-1, keepdims=True)) + epsilon) * norm_gain
    gate_heads = jax.nn.silu(gate_lin.reshape(length, head_count, -1))
    return (normed * gate_heads * inside[:, None, None]).reshape(length, -1)

def rms_scale(values):
    return lax.rsqrt(lax.optimization_barrier(jnp.mean(values * values, axis=1)) + epsilon)

def rms_backward(values, row_scale, gain_vector, upstream):
    weighted = upstream * gain_vector
    inner_mean = lax.optimization_barrier(jnp.mean(weighted * values, axis=1))
    grad_values = row_scale[:, None] * weighted - values * (row_scale * row_scale * row_scale * inner_mean)[:, None]
    return (grad_values, lax.optimization_barrier(jnp.sum(upstream * values * row_scale[:, None], axis=0)))

def matmul(left, right):
    return jnp.dot(left.astype(jnp.float32), right.astype(jnp.float32), preferred_element_type=jnp.float32)

def left_matmul_result(left, right):
    return jnp.dot(left.T.astype(jnp.float32), right.astype(jnp.float32), preferred_element_type=jnp.float32)

def right_product(left, right):
    return jnp.dot(left.astype(jnp.float32), right.T.astype(jnp.float32), preferred_element_type=jnp.float32)

def reference(block_input, attn_gain, query_weight, key_weight, value_weight, gate_weight, decay_weight, beta_weight, query_conv, key_conv, value_conv, decay_log, decay_bias, head_gain, out_weight, ffn_gain, ffn_gate, ffn_up, ffn_down, out_grad, seq_starts, seq_lengths):
    slot_count = seq_starts.shape[0]
    slot_rows = block_input.shape[0] // slot_count
    feature_count = block_input.shape[1]
    in_weights = (query_weight, key_weight, value_weight, gate_weight, decay_weight, beta_weight)
    mixer_params = (query_conv, key_conv, value_conv, decay_log, decay_bias, head_gain)
    templates = (attn_gain,) + in_weights + mixer_params + (out_weight, ffn_gain, ffn_gate, ffn_up, ffn_down)
    initial = tuple((jnp.zeros(template.shape, jnp.float32) for template in templates))

    def one_slot(grand_totals, slot_data):
        rows_in, row_gradients, starts, lengths = slot_data
        segment, inside = segment_info(starts, lengths, slot_rows)
        inputs = rows_in.astype(jnp.float32)
        first_scale = rms_scale(inputs)
        first_normalized = (inputs * first_scale[:, None] * attn_gain).astype(jnp.bfloat16)
        linears = tuple((matmul(first_normalized, weight) for weight in in_weights))

        def mixer_piece(linear_set, param_set):
            return token_mixer(linear_set, param_set, segment, inside)
        gated, mixer_back = jax.vjp(mixer_piece, linears, mixer_params)
        mixer_output = gated.astype(jnp.bfloat16)
        resid = inputs + matmul(mixer_output, out_weight)
        second_scale = rms_scale(resid)
        second_normalized = (resid * second_scale[:, None] * ffn_gain).astype(jnp.bfloat16)
        gate_part = matmul(second_normalized, ffn_gate)
        up_part = matmul(second_normalized, ffn_up)
        hidden_activation = (jax.nn.silu(gate_part) * up_part * inside[:, None]).astype(jnp.bfloat16)
        output = (resid + matmul(hidden_activation, ffn_down)).astype(jnp.bfloat16)
        grad_hidden = right_product(row_gradients, ffn_down) * inside[:, None]
        sigmoid_gate = jax.nn.sigmoid(gate_part)
        gate_gradient = (grad_hidden * up_part * sigmoid_gate * (1.0 + gate_part * (1.0 - sigmoid_gate))).astype(jnp.bfloat16)
        up_gradient = (grad_hidden * gate_part * sigmoid_gate).astype(jnp.bfloat16)
        grad_second = right_product(gate_gradient, ffn_gate) + right_product(up_gradient, ffn_up)
        resid_part, feedforward_gain_share = rms_backward(resid, second_scale, ffn_gain, grad_second)
        grad_resid = row_gradients.astype(jnp.float32) + resid_part
        residual_signal_path = grad_resid.astype(jnp.bfloat16)
        grad_mixed = right_product(residual_signal_path, out_weight)
        grad_linears, parameter_gradients = mixer_back(grad_mixed)
        linear_signal_path = tuple((gradient.astype(jnp.bfloat16) for gradient in grad_linears))
        grad_first = right_product(linear_signal_path[0], in_weights[0])
        for signal_path_gradient, weight in zip(linear_signal_path[1:], in_weights[1:]):
            grad_first = grad_first + right_product(signal_path_gradient, weight)
        input_part, attention_gain_share = rms_backward(inputs, first_scale, attn_gain, grad_first)
        input_grad = grad_resid + input_part
        summand_terms = (attention_gain_share,) + tuple((left_matmul_result(first_normalized, signal_path_gradient) for signal_path_gradient in linear_signal_path)) + tuple(parameter_gradients) + (left_matmul_result(mixer_output, residual_signal_path), feedforward_gain_share, left_matmul_result(second_normalized, gate_gradient), left_matmul_result(second_normalized, up_gradient), left_matmul_result(hidden_activation, row_gradients))
        grand_totals = tuple((running_total + summand_term for running_total, summand_term in zip(grand_totals, summand_terms)))
        return (grand_totals, (output, input_grad))
    slot_inputs = block_input.reshape(slot_count, slot_rows, feature_count)
    slot_grads = out_grad.reshape(slot_count, slot_rows, feature_count)
    grand_totals, stacked = lax.scan(one_slot, initial, (slot_inputs, slot_grads, seq_starts, seq_lengths))
    output = stacked[0].reshape(-1, feature_count)
    input_grad = stacked[1].reshape(-1, feature_count)
    return (output, input_grad, grand_totals[0], grand_totals[1], grand_totals[2], grand_totals[3], grand_totals[4], grand_totals[5], grand_totals[6], grand_totals[7], grand_totals[8], grand_totals[9], grand_totals[10], grand_totals[11], grand_totals[12], grand_totals[13], grand_totals[14], grand_totals[15], grand_totals[16], grand_totals[17])
```

```python
import functools
import types

import jax
import jax.numpy as jnp
from jax import lax
from jax.experimental import pallas as pl
from jax.experimental.pallas import tpu as pltpu
from jax.sharding import PartitionSpec as P

epsilon = 1e-06
highest = lax.Precision.HIGHEST


def fp_dot(left, right, left_dim, right_dim):
    return lax.dot_general(
        left,
        right,
        (((left_dim,), (right_dim,)), ((), ())),
        precision=highest,
        preferred_element_type=jnp.float32,
    )


def plain_softplus(values):
    return jnp.maximum(values, 0.0) + jnp.log1p(jnp.exp(-jnp.abs(values)))


@jax.custom_vjp
def smooth_ramp(values):
    return plain_softplus(values)


smooth_ramp.defvjp(
    lambda values: (plain_softplus(values), values),
    lambda values, upstream: (upstream * lax.logistic(values),),
)


@jax.custom_vjp
def apply_inverse(inverse, lower_part, target):
    return fp_dot(inverse, target, 1, 0)


def apply_inverse_forward(inverse, lower_part, target):
    writes = fp_dot(inverse, target, 1, 0)
    return writes, (inverse, writes)


def apply_inverse_backward(saved, upstream):
    inverse, writes = saved
    grad_target = fp_dot(inverse, upstream, 0, 0)
    return (jnp.zeros_like(inverse), -fp_dot(grad_target, writes, 1, 1), grad_target)


apply_inverse.defvjp(apply_inverse_forward, apply_inverse_backward)


def unit_lower_inverse(lower_part, row_index, column_index):
    length = lower_part.shape[0]
    inverse = jnp.where(row_index == column_index, 1.0, 0.0)
    level = 0
    while (1 << level) < length:
        row_block = row_index >> level
        column_block = column_index >> level
        joined = (row_block == column_block + 1) & ((column_block & 1) == 0)
        corner = jnp.where(joined, lower_part, 0.0)
        if level == 0:
            inverse = inverse - corner
        else:
            inverse = inverse - fp_dot(fp_dot(inverse, corner, 1, 0), inverse, 1, 0)
        level += 1
    return inverse


def slot_masks(bounds, length, tap_count):
    row_index = lax.broadcasted_iota(jnp.int32, (length, length), 0)
    column_index = lax.broadcasted_iota(jnp.int32, (length, length), 1)
    token = lax.broadcasted_iota(jnp.int32, (length, 1), 0)
    row_segment = jnp.zeros((length, length), jnp.int32)
    column_segment = jnp.zeros((length, length), jnp.int32)
    inside = jnp.zeros((length, 1), jnp.float32)
    for begin, count in zip(*bounds):
        end = begin + count
        row_segment += jnp.where(row_index >= begin, 1, 0) + jnp.where(row_index >= end, 1, 0)
        column_segment += jnp.where(column_index >= begin, 1, 0)
        column_segment += jnp.where(column_index >= end, 1, 0)
        inside += jnp.where((token >= begin) & (token < end), 1.0, 0.0)
    same = row_segment == column_segment
    shifts = [
        jnp.where(same & (column_index == row_index - offset), 1.0, 0.0)
        for offset in range(1, tap_count)
    ]
    return dict(
        row_index=row_index,
        column_index=column_index,
        shifts=shifts,
        strict=jnp.where(same & (row_index > column_index), 1.0, 0.0),
        within=jnp.where(same & (row_index >= column_index), 1.0, 0.0),
        upto=jnp.where(row_index >= column_index, 1.0, 0.0),
        later=jnp.where(row_index > column_index, 1.0, 0.0),
        inside=inside,
    )


def conv_head(signal, taps, shifts):
    total = taps[-1] * signal
    for offset, shift in enumerate(shifts, 1):
        total = total + taps[len(taps) - 1 - offset] * fp_dot(shift, signal, 1, 0)
    return total * lax.logistic(total)


def unit_rows(values):
    return values * lax.rsqrt(jnp.sum(values * values, axis=1, keepdims=True) + epsilon)


def mixer_head(masks, inverse, bias, linears, taps, rate, norm_gain):
    query_lin, key_lin, value_lin, gate_lin, decay_lin, rate_lin = linears
    differentiated = inverse is not None
    queries = unit_rows(conv_head(query_lin, taps[0], masks["shifts"]))
    queries = queries * queries.shape[1] ** (-0.5)
    keys = unit_rows(conv_head(key_lin, taps[1], masks["shifts"]))
    values = conv_head(value_lin, taps[2], masks["shifts"])
    write_rate = lax.logistic(rate_lin)
    ramp = smooth_ramp if differentiated else plain_softplus
    log_decay = -rate * ramp(decay_lin + bias)
    ratio = jnp.exp(fp_dot(masks["upto"], log_decay * masks["later"], 1, 0))
    lower_part = write_rate * ratio * fp_dot(keys, keys, 1, 1) * masks["strict"]
    target = write_rate * values
    if differentiated:
        writes = apply_inverse(inverse, lower_part, target)
    else:
        inverse = unit_lower_inverse(lower_part, masks["row_index"], masks["column_index"])
        writes = fp_dot(inverse, target, 1, 0)
    heads = fp_dot(ratio * fp_dot(queries, keys, 1, 1) * masks["within"], writes, 1, 0)
    mean_square = jnp.sum(heads * heads, axis=1, keepdims=True) * (1.0 / heads.shape[1])
    normed = heads * lax.rsqrt(mean_square + epsilon) * norm_gain
    gated = normed * (gate_lin * lax.logistic(gate_lin)) * masks["inside"]
    return (gated, inverse)


LANES = 128
MESH = pl.DeviceIdType.MESH


def head_operands(h, heads, lin_ref, conv_refs, log_ref, bias_ref, gain_ref):
    length = lin_ref.shape[0]
    key_size = conv_refs[0].shape[1] // heads
    value_size = conv_refs[2].shape[1] // heads
    widths = (key_size, key_size, value_size, value_size)
    spans = []
    base = 0
    for width in widths:
        spans.append(slice(base + h * width, base + (h + 1) * width))
        base += heads * width
    tail = lin_ref[:, base : base + LANES]
    lane = lax.broadcasted_iota(jnp.int32, tail.shape, 1)
    columns = [
        jnp.sum(jnp.where(lane == place, tail, 0.0), axis=1, keepdims=True)
        for place in (h, heads + h)
    ]
    linears = tuple(lin_ref[:, span] for span in spans) + tuple(columns)
    tap_spans = [slice(h * width, (h + 1) * width) for width in widths[:3]]
    taps = tuple(
        tuple(ref[i : i + 1, span] for i in range(ref.shape[0]))
        for ref, span in zip(conv_refs, tap_spans)
    )
    rate = jnp.exp(jnp.full((length, 1), log_ref[h], jnp.float32))
    bias = jnp.full((length, 1), bias_ref[h], jnp.float32)
    return linears, taps, rate, bias, gain_ref[...], spans, tap_spans, base


def spread_columns(columns):
    shape = (columns[0].shape[0], LANES)
    lane = lax.broadcasted_iota(jnp.int32, shape, 1)
    total = jnp.zeros(shape, jnp.float32)
    for place, column in enumerate(columns):
        total = total + jnp.where(lane == place, column, 0.0)
    return total


def wrap(index, count):
    return lax.rem(index, count)


def dot_nn(left, right):
    return lax.dot_general(
        left, right, (((1,), (0,)), ((), ())), preferred_element_type=jnp.float32
    )


def dot_nt(left, right):
    return lax.dot_general(
        left, right, (((1,), (1,)), ((), ())), preferred_element_type=jnp.float32
    )


def dot_tn(left, right):
    return lax.dot_general(
        left, right, (((0,), (0,)), ((), ())), preferred_element_type=jnp.float32
    )


def diagonal(length):
    row = lax.broadcasted_iota(jnp.int32, (length, length), 0)
    column = lax.broadcasted_iota(jnp.int32, (length, length), 1)
    return row == column


def as_row(column):
    length = column.shape[0]
    return jnp.sum(jnp.where(diagonal(length), column, 0.0), axis=0, keepdims=True)


def as_column(row):
    length = row.shape[1]
    return jnp.sum(jnp.where(diagonal(length), row, 0.0), axis=1, keepdims=True)


class Link:
    def __init__(self, axis, count, me, landing, sems, place):
        self.axis, self.count, self.me = axis, count, me
        self.landing, self.sems, self.place = landing, sems, place
        self.source = None

    def copy(self, source, target, slot):
        return pltpu.make_async_remote_copy(
            src_ref=source,
            dst_ref=self.landing.at[slot],
            send_sem=self.sems.at[self.place, 0, target],
            recv_sem=self.sems.at[self.place, 1, slot],
            device_id={self.axis: target},
            device_id_type=MESH,
        )

    def send(self, source, target):
        self.copy(source, target, self.me).start()

    def spread(self):
        source = self.landing.at[self.me]
        for k in range(1, self.count):
            self.send(source, wrap(self.me + k, self.count))

    def arrive(self, slot):
        self.copy(self.landing.at[slot], slot, slot).wait_recv()

    def drain(self):
        for k in range(1, self.count):
            target = wrap(self.me + k, self.count)
            source = self.landing.at[self.me] if self.source is None else self.source.at[target]
            self.copy(source, target, self.me).wait_send()


def block_kernel(sizes, names, *flat):
    ref = types.SimpleNamespace(**dict(zip(names, flat)))
    groups, rows, cols, heads, features = sizes
    d, r, c = lax.axis_index("dp"), lax.axis_index("row"), lax.axis_index("col")
    sems, far_sems, dp_sems = ref.sems, ref.far_sems, ref.dp_sems
    grid_sems, half_sems = ref.grid_sems, ref.half_sems
    spread_count = groups * cols
    mine = d * cols + c

    barrier = pltpu.get_barrier_semaphore()
    for k in range(1, rows):
        pl.semaphore_signal(
            barrier, inc=1, device_id={"row": wrap(r + k, rows)}, device_id_type=MESH
        )

    def greet(k, carry):
        other = wrap(mine + k, spread_count)
        pl.semaphore_signal(
            barrier,
            inc=1,
            device_id={"dp": other // cols, "col": wrap(other, cols)},
            device_id_type=MESH,
        )
        return carry

    lax.fori_loop(1, spread_count, greet, 0)
    pl.semaphore_wait(barrier, rows - 1 + spread_count - 1)

    links = []

    def link_row(landing):
        links.append(Link("row", rows, r, landing, sems, len(links)))
        return links[-1]

    def link_col(landing):
        links.append(Link("col", cols, c, landing, sems, len(links)))
        return links[-1]

    x_link, og_link = link_col(ref.xng), link_row(ref.og4.at[c])
    b_link, ss1_link = link_row(ref.xr), link_row(ref.ss1_recv)
    mix_link, d_link = link_row(ref.mixg), link_col(ref.d_recv)
    n2_link, ss2_link = link_row(ref.n24.at[c]), link_row(ref.ss2_recv)
    wg_link = link_row(ref.pair_ffn.at[0])
    i_link, o_link = link_row(ref.i_recv), link_row(ref.o_recv)
    t2c_link, t2_link = link_col(ref.t2c_recv), link_row(ref.t2g)
    gr_link, k_link = link_col(ref.grg), link_row(ref.k_recv)
    l_link, t1_link = link_row(ref.lg), link_row(ref.t1g)
    m_link, t1c_link = link_col(ref.m_recv), link_col(ref.t1_recv)
    p_link = link_row(ref.p_recv)

    def grid_copy(place, source, landing, target, slot, j):
        return pltpu.make_async_remote_copy(
            src_ref=source,
            dst_ref=landing.at[slot, j],
            send_sem=grid_sems.at[place, 0, target, j],
            recv_sem=grid_sems.at[place, 1, slot, j],
            device_id={"col": target},
            device_id_type=MESH,
        )

    halves = (d,) if groups == 2 else (0, 1)
    half_sent = []

    def half_copy(place, hop, source, landing, target, slot, half, peer):
        return pltpu.make_async_remote_copy(
            src_ref=source,
            dst_ref=landing.at[slot, half],
            send_sem=half_sems.at[place, hop, 0, target, half],
            recv_sem=half_sems.at[place, hop, 1, slot, half],
            device_id=peer,
            device_id_type=MESH,
        )

    def weights_out(place, source, landing):
        for k in range(1, rows):
            t = wrap(r + k, rows)
            for half in halves:
                copy = half_copy(place, 0, source(t, half), landing, t, r, half, {"row": t})
                copy.start()
                half_sent.append(copy)

    def weights_across(place, landing):
        for k in range(1, rows):
            j = wrap(r + k, rows)
            for half in halves:
                here = landing.at[j, half]
                half_copy(place, 0, here, landing, j, j, half, {"row": j}).wait_recv()
                if groups == 2:
                    copy = half_copy(place, 1, here, landing, j, j, half, {"dp": 1 - d})
                    copy.start()
                    half_sent.append(copy)

    def weights_in(place, landing):
        if groups == 2:
            for k in range(1, rows):
                j = wrap(r + k, rows)
                here = landing.at[j, 1 - d]
                half_copy(place, 1, here, landing, j, j, 1 - d, {"dp": 1 - d}).wait_recv()

    grid_sent = []

    def grid_send(place, source, landing, target, j):
        copy = grid_copy(place, source, landing, target, c, j)
        copy.start()
        grid_sent.append(copy)

    def grid_arrive(place, landing, slot, j):
        grid_copy(place, landing.at[slot, j], landing, slot, slot, j).wait_recv()

    def onward(row_link, place, blocks):
        for k in range(rows):
            j = gathered(row_link, k)
            for step in range(1, cols):
                grid_send(place, blocks.at[c, j], blocks, wrap(c + step, cols), j)

    def gathered(link_used, k):
        slot = wrap(link_used.me + k, link_used.count)
        if k:
            link_used.arrive(slot)
        return slot

    def pass_on(link_used, send, target):
        link_used.source = send

        @pl.when(target != link_used.me)
        def _():
            link_used.send(send.at[target], target)

    def total(link_used, send):
        running = send[link_used.me].astype(jnp.float32)
        for k in range(1, link_used.count):
            slot = wrap(link_used.me + k, link_used.count)
            link_used.arrive(slot)
            running = running + link_used.landing[slot].astype(jnp.float32)
        return running

    bf16 = jnp.bfloat16

    ref.og4[c, r] = ref.out_grad[...]

    def send_squares(link_used, values):
        sums = link_used.landing
        sums[r, 0:1, :] = as_row(jnp.sum(values * values, axis=1, keepdims=True))
        link_used.spread()

    def row_scale(link_used):
        sums = link_used.landing
        for k in range(1, rows):
            link_used.arrive(wrap(r + k, rows))
        running = sums[0, 0:1, :]
        for j in range(1, rows):
            running = running + sums[j, 0:1, :]
        return lax.rsqrt(as_column(running) * (1.0 / features) + epsilon)

    gain1 = ref.gain1[...]
    gain2 = ref.gain2[...]
    inputs = ref.x[...].astype(jnp.float32)
    send_squares(ss1_link, inputs)
    in_refs = (ref.wq, ref.wk, ref.wv, ref.wg, ref.wt)
    in_spans = []
    base = 0
    depth = ref.w_all.shape[2]
    for weight in in_refs:
        width = weight.shape[1]
        in_spans.append(slice(base, base + width))
        base += width
        for half in range(2):
            ref.w_all[r, half, :, in_spans[-1]] = weight[half * depth : (half + 1) * depth, :]
    scale1 = row_scale(ss1_link)
    weights_out(0, lambda t, half: ref.w_all.at[r, half], ref.w_all)
    ref.xng[c] = (inputs * scale1 * gain1).astype(bf16)
    x_link.spread()
    for k in range(cols):
        t = gathered(x_link, k)
        pass_on(b_link, ref.xng, t)
    og_link.spread()

    width, hidden = ref.gate.shape
    part = hidden // rows
    identity = jnp.where(diagonal(width), 1.0, 0.0).astype(bf16)
    for place, weight in enumerate((ref.gate, ref.up)):
        turned = dot_tn(weight[...], identity)
        for j in range(rows):
            for half in range(2):
                ref.ffn_send[j, half, place * part : (place + 1) * part, :] = turned[
                    j * part : (j + 1) * part, half * depth : (half + 1) * depth
                ].astype(bf16)
    for j in range(rows):
        for half in range(2):
            ref.ffn_send[j, half, 2 * part : 3 * part, :] = ref.down[
                j * part : (j + 1) * part, half * depth : (half + 1) * depth
            ]
    weights_out(1, lambda t, half: ref.ffn_send.at[t, half], ref.ffn_all)
    ref.ffn_all[r] = ref.ffn_send[r]

    def share(j, span):
        return jnp.concatenate([ref.ffn_all[j, half, span, :] for half in range(2)], axis=1)


    def row_total(link_used, send):
        running = send[link_used.me, 0:1, :]
        for k in range(1, link_used.count):
            slot = wrap(link_used.me + k, link_used.count)
            link_used.arrive(slot)
            running = running + link_used.landing[slot, 0:1, :]
        return running

    ref.xr[r] = ref.xng[r]
    weights_across(0, ref.w_all)
    for k in range(1, rows):
        b_link.arrive(wrap(r + k, rows))
    weights_in(0, ref.w_all)
    for span in in_spans:
        ref.lin[:, span] = sum(
            dot_nn(ref.xr[j], ref.w_all[j, :, :, span].reshape(2 * depth, span.stop - span.start))
            for j in range(rows)
        )
    lin_ref = ref.lin
    length = lin_ref.shape[0]
    conv_refs = (ref.qc, ref.kc, ref.vc)
    slot_index = d * cols + r
    starts = [ref.starts[slot_index, i] for i in range(ref.starts.shape[1])]
    counts = [ref.counts[slot_index, i] for i in range(ref.counts.shape[1])]
    masks = slot_masks((starts, counts), length, conv_refs[0].shape[0])
    for h in range(heads):
        linears, taps, rate, bias, gain, _, tap_spans, _ = head_operands(
            h, heads, lin_ref, conv_refs, ref.log, ref.bias, ref.norm_gain
        )
        gated, inverse = mixer_head(masks, None, bias, linears, taps, rate, gain)
        ref.mixg[r, :, tap_spans[2]] = gated.astype(bf16)
        ref.inverse[h] = inverse
    mix_link.spread()
    for k in range(rows):
        t = gathered(mix_link, k)
        ref.d_send[t] = dot_nn(ref.mixg[t], ref.wo[...])
        pass_on(d_link, ref.d_send, t)
    onward(og_link, 0, ref.og4)
    weights_across(1, ref.ffn_all)
    resid = inputs + total(d_link, ref.d_send)
    ref.resid[...] = resid
    send_squares(ss2_link, resid)
    scale2 = row_scale(ss2_link)
    ref.n24[c, r] = (resid * scale2 * gain2).astype(bf16)
    n2_link.spread()
    onward(n2_link, 1, ref.n24)

    weights_in(1, ref.ffn_all)
    token = lax.broadcasted_iota(jnp.int32, (length, 1), 0)
    places = [slice(i * part, (i + 1) * part) for i in range(3)]
    for k in range(cols):
        t = wrap(c + k, cols)
        if k:
            for j in range(rows):
                grid_arrive(0, ref.og4, t, j)
            for j in range(rows):
                grid_arrive(1, ref.n24, t, j)
        gate_part, up_part, grad_hidden = (
            sum(dot_nt(tokens[t, j], share(j, span)) for j in range(rows))
            for tokens, span in zip((ref.n24, ref.n24, ref.og4), places)
        )
        inside = jnp.zeros((length, 1), jnp.float32)
        for i in range(ref.starts.shape[1]):
            begin = ref.starts[d * cols + t, i]
            end = begin + ref.counts[d * cols + t, i]
            inside += jnp.where((token >= begin) & (token < end), 1.0, 0.0)
        grad_hidden = grad_hidden * inside
        sigmoid = lax.logistic(gate_part)
        ref.hid[t] = (gate_part * sigmoid * up_part * inside).astype(bf16)
        grad_gate = grad_hidden * up_part * sigmoid * (1.0 + gate_part * (1.0 - sigmoid))
        grad_up = grad_hidden * gate_part * sigmoid
        ref.gg[t] = grad_gate.astype(bf16)
        ref.gu[t] = grad_up.astype(bf16)
        inner_sum = jnp.sum(grad_gate * gate_part + grad_up * up_part, axis=1, keepdims=True)
        ref.t2_send[t, 0:1, :] = as_row(inner_sum)
        pass_on(t2c_link, ref.t2_send, t)

    def all_tokens(source):
        block = source[...]
        return block.reshape(block.shape[0] * block.shape[1], block.shape[2])

    def feature_sums(place, send, landing, grads):
        for k in range(1, rows + 1):
            j = wrap(r + k, rows)
            terms = sum(dot_nn(grad, share(j, span)) for grad, span in grads)
            for t in range(cols):
                send[t, j] = terms[t * length : (t + 1) * length].astype(bf16)
            for step in range(1, cols):
                t = wrap(c + step, cols)
                grid_send(place, send.at[t, j], landing, t, j)

    def across_rows(place, send, landing, row_link, row_send):
        for k in range(1, rows + 1):
            j = wrap(r + k, rows)
            running = send[c, j].astype(jnp.float32)
            for step in range(1, cols):
                t = wrap(c + step, cols)
                grid_arrive(place, landing, t, j)
                running = running + landing[t, j].astype(jnp.float32)
            row_send[j] = running.astype(bf16)
            pass_on(row_link, row_send, j)

    feature_sums(
        2, ref.gi_send, ref.gi_recv,
        ((all_tokens(ref.gg), places[0]), (all_tokens(ref.gu), places[1])),
    )
    ref.t2g[r, 0:1, :] = row_total(t2c_link, ref.t2_send)
    t2_link.spread()
    across_rows(2, ref.gi_send, ref.gi_recv, i_link, ref.i_send)
    feature_sums(3, ref.go_send, ref.go_recv, ((all_tokens(ref.hid), places[2]),))

    dp_copies = []

    def trade(pair, part):
        if groups == 2:
            copy = pltpu.make_async_remote_copy(
                src_ref=pair.at[0],
                dst_ref=pair.at[1],
                send_sem=dp_sems.at[part, 0],
                recv_sem=dp_sems.at[part, 1],
                device_id={"dp": 1 - d},
                device_id_type=MESH,
            )
            copy.start()
            dp_copies.append(copy)

    grad_second = total(i_link, ref.i_send) * scale2
    t2 = as_column(row_total(t2_link, ref.t2g)) * scale2 * scale2 * (1.0 / features)
    resid = ref.resid[...]
    grad_resid = ref.out_grad[...].astype(jnp.float32) + grad_second * gain2 - resid * t2
    ref.grad_resid[...] = grad_resid
    ref.grg[c] = grad_resid.astype(bf16)
    gr_link.spread()
    ffn_gain_part = jnp.sum(grad_second * resid, axis=0, keepdims=True)

    across_rows(3, ref.go_send, ref.go_recv, o_link, ref.o_send)
    for k in range(cols):
        t = gathered(gr_link, k)
        ref.k_send[t] = dot_nt(ref.grg[t], ref.wo[...]).astype(bf16)
        pass_on(k_link, ref.k_send, t)
    sides = ((ref.gg, ref.n24), (ref.gu, ref.n24), (ref.hid, ref.og4))
    lefts = [all_tokens(left) for left, _ in sides]
    for k in range(1, rows + 1):
        j = wrap(r + k, rows)
        for span, left, (_, right) in zip(places, lefts, sides):
            tokens = right[:, j].reshape(cols * length, width)
            ref.wg_send[j, span, :] = dot_tn(left, tokens).astype(bf16)
        pass_on(wg_link, ref.wg_send, j)
    ref.pair_ffn[0, r] = ref.wg_send[r]
    ref.pair_out[0] = dot_tn(all_tokens(ref.mixg), all_tokens(ref.grg)).astype(bf16)
    trade(ref.pair_out, 0)
    ref.output[...] = (ref.resid[...] + total(o_link, ref.o_send)).astype(bf16)

    ref.upstream[...] = total(k_link, ref.k_send)
    masks = slot_masks((starts, counts), length, conv_refs[0].shape[0])
    decay_columns, rate_columns, log_columns = [], [], []
    gain_total = jnp.zeros(ref.norm_gain.shape, jnp.float32)
    inner_sum = jnp.zeros((length, 1), jnp.float32)
    params = ref.p_recv
    params[r] = jnp.zeros(params.shape[1:], jnp.float32)
    taps_count = conv_refs[0].shape[0]
    key_width = conv_refs[0].shape[1]
    for h in range(heads):
        linears, taps, rate, bias, gain, spans, tap_spans, tail_base = head_operands(
            h, heads, lin_ref, conv_refs, ref.log, ref.bias, ref.norm_gain
        )
        inverse = ref.inverse[h]

        def piece(linear_set, tap_set, rate_set, gain_set):
            return mixer_head(masks, inverse, bias, linear_set, tap_set, rate_set, gain_set)[0]

        _, back = jax.vjp(piece, linears, taps, rate, gain)
        grad_linears, grad_taps, grad_rate, grad_gain = back(ref.upstream[:, tap_spans[2]])
        for span, grad, linear in zip(spans, grad_linears, linears):
            ref.lg[r, :, span] = grad.astype(bf16)
        for grad, linear in zip(grad_linears, linears):
            inner_sum = inner_sum + jnp.sum(grad * linear, axis=1, keepdims=True)
        places = ((taps_count, 0), (taps_count, key_width), (0, 0))
        for (top, left), span, grads in zip(places, tap_spans, grad_taps):
            for i, grad in enumerate(grads):
                params[r, top + i : top + i + 1, left + span.start : left + span.stop] = grad
        gain_total = gain_total + grad_gain
        decay_columns.append(grad_linears[4])
        rate_columns.append(grad_linears[5])
        log_columns.append(grad_rate * rate)
    tails = spread_columns(decay_columns + rate_columns)
    ref.lg[r, :, tail_base : tail_base + LANES] = tails.astype(bf16)
    l_link.spread()
    for k in range(1, rows):
        wg_link.arrive(wrap(r + k, rows))
    trade(ref.pair_ffn, 1)
    ref.t1g[r, 0:1, :] = as_row(inner_sum)
    t1_link.spread()
    value_size = gain_total.shape[1]
    params[r, 2 * taps_count : 2 * taps_count + 1, 0:value_size] = gain_total
    params[r, 2 * taps_count + 1 : 2 * taps_count + 2, 0:LANES] = jnp.sum(
        spread_columns(log_columns + decay_columns), axis=0, keepdims=True
    )
    p_link.spread()

    for k in range(rows):
        t = gathered(t1_link, k)
        pass_on(t1c_link, ref.t1g, t)
        gathered(l_link, k)
        terms = dot_nt(ref.lg[t, :, in_spans[0]], in_refs[0][...])
        for weight, span in zip(in_refs[1:], in_spans[1:]):
            terms = terms + dot_nt(ref.lg[t, :, span], weight[...])
        ref.m_send[t] = terms.astype(bf16)
        pass_on(m_link, ref.m_send, t)
    first_all = all_tokens(ref.xng)
    for part, span in enumerate(in_spans):
        grads = ref.lg[:, :, span]
        grads = grads.reshape(grads.shape[0] * grads.shape[1], grads.shape[2])
        ref.pair_in[0, :, span] = dot_tn(first_all, grads).astype(bf16)
    trade(ref.pair_in, 2)

    for k in range(1, rows):
        p_link.arrive(wrap(r + k, rows))
    summed = params[0]
    for j in range(1, rows):
        summed = summed + params[j]
    far_p, far_g = ref.far_p, ref.far_g
    far_p[d] = summed

    def far_copy(landing, place, slot, target, peer):
        return pltpu.make_async_remote_copy(
            src_ref=landing.at[slot],
            dst_ref=landing.at[slot],
            send_sem=far_sems.at[place, 0, target],
            recv_sem=far_sems.at[place, 1, slot],
            device_id=peer,
            device_id_type=MESH,
        )

    def dp_peers(act):
        def step(k, carry):
            other = wrap(d + k, groups)
            act(other, {"dp": other})
            return carry

        lax.fori_loop(1, groups, step, 0)

    def far_peers(act):
        def step(k, carry):
            other = wrap(mine + k, spread_count)
            act(other, {"dp": other // cols, "col": wrap(other, cols)})
            return carry

        lax.fori_loop(1, spread_count, step, 0)

    dp_peers(lambda other, peer: far_copy(far_p, 0, d, other, peer).start())

    grad_first = total(m_link, ref.m_send) * scale1
    t1 = as_column(row_total(t1c_link, ref.t1g)) * scale1 * scale1 * (1.0 / features)
    ref.input_grad[...] = ref.grad_resid[...] + grad_first * gain1 - inputs * t1
    far_g[mine] = jnp.zeros(far_g.shape[1:], jnp.float32)
    far_g[mine, 0:1, :] = jnp.sum(grad_first * inputs, axis=0, keepdims=True)
    far_g[mine, 1:2, :] = ffn_gain_part
    far_g[mine, 2:3, 0:value_size] = summed[2 * taps_count : 2 * taps_count + 1, 0:value_size]
    far_peers(lambda other, peer: far_copy(far_g, 1, mine, other, peer).start())
    dp_peers(lambda other, peer: far_copy(far_p, 0, other, other, peer).wait_recv())
    far_peers(lambda other, peer: far_copy(far_g, 1, other, other, peer).wait_recv())
    ref.params[...] = lax.fori_loop(1, groups, lambda j, acc: acc + far_p[j], far_p[0])
    ref.gains[...] = lax.fori_loop(1, spread_count, lambda j, acc: acc + far_g[j], far_g[0])
    for copy in dp_copies:
        copy.wait_recv()

    dp_peers(lambda other, peer: far_copy(far_p, 0, d, other, peer).wait_send())
    far_peers(lambda other, peer: far_copy(far_g, 1, mine, other, peer).wait_send())
    for copy in dp_copies:
        copy.wait_send()
    for copy in grid_sent + half_sent:
        copy.wait_send()
    for used in links:
        used.drain()


def finish_kernel(heads, taps_count, *refs):
    (pair_in, pair_out, pair_ffn, params, gains, out_in, grad_in) = refs[:7]
    (output, input_grad, attn, gq, gk, gv, gg, gd, gb, cq, ck, cv, dl, db, hg, go, fg, gate, up, down) = refs[7:]

    def both(pair, *index):
        return pair[(0,) + index].astype(jnp.float32) + pair[(1,) + index].astype(jnp.float32)

    output[...] = out_in[...]
    input_grad[...] = grad_in[...]
    attn[...] = gains[0:1, :]
    fg[...] = gains[1:2, :]
    hg[...] = gains[2:3, 0 : hg.shape[1]]
    base = 0
    every = slice(None)
    for ref in (gq, gk, gv, gg):
        width = ref.shape[1]
        ref[...] = both(pair_in, every, slice(base, base + width))
        base += width
    tail = both(pair_in, every, slice(base, base + LANES))
    gd[...] = tail[:, 0:heads]
    gb[...] = tail[:, heads : 2 * heads]
    key_width = cq.shape[1]
    cv[...] = params[0:taps_count, :]
    cq[...] = params[taps_count : 2 * taps_count, 0:key_width]
    ck[...] = params[taps_count : 2 * taps_count, key_width : 2 * key_width]
    dl[...] = params[2 * taps_count + 1 : 2 * taps_count + 2, 0:heads]
    db[...] = params[2 * taps_count + 1 : 2 * taps_count + 2, heads : 2 * heads]
    go[...] = both(pair_out)
    rows, part = pair_ffn.shape[1], pair_ffn.shape[2] // 3
    identity = jnp.where(diagonal(gate.shape[0]), 1.0, 0.0).astype(jnp.bfloat16)

    def units(group, place):
        blocks = [pair_ffn[group, j, place * part : (place + 1) * part, :] for j in range(rows)]
        return jnp.concatenate(blocks, axis=0)

    for place, ref in enumerate((gate, up)):
        ref[...] = dot_nt(identity, units(0, place)) + dot_nt(identity, units(1, place))
    for j in range(rows):
        down[j * part : (j + 1) * part, :] = both(pair_ffn, j, slice(2 * part, 3 * part))


def shards(
    block_input,
    attn_gain,
    query_weight,
    key_weight,
    value_weight,
    gate_weight,
    decay_weight,
    beta_weight,
    query_conv,
    key_conv,
    value_conv,
    decay_log,
    decay_bias,
    head_gain,
    out_weight,
    ffn_gain,
    ffn_gate,
    ffn_up,
    ffn_down,
    out_grad,
    seq_starts,
    seq_lengths,
):
    groups, rows, cols = (lax.axis_size(name) for name in ("dp", "row", "col"))
    length, width = block_input.shape
    heads = decay_log.shape[0]
    taps_count = query_conv.shape[0]
    keys, values = query_weight.shape[1], value_weight.shape[1]
    hidden = ffn_gate.shape[1]
    part = hidden // rows
    tail_weight = jnp.concatenate([decay_weight, beta_weight], axis=1)
    tail_weight = jnp.pad(tail_weight, ((0, 0), (0, LANES - tail_weight.shape[1])))
    in_width = 2 * keys + 2 * values + LANES
    bf16, f32 = jnp.bfloat16, jnp.float32
    smem = pl.BlockSpec(memory_space=pltpu.SMEM)
    vmem = pl.BlockSpec(memory_space=pltpu.VMEM)
    operands = dict(
        starts=seq_starts, counts=seq_lengths, log=decay_log, bias=decay_bias,
        x=block_input, gain1=attn_gain[None, :], wq=query_weight, wk=key_weight,
        wv=value_weight, wg=gate_weight, wt=tail_weight, qc=query_conv, kc=key_conv,
        vc=value_conv, norm_gain=head_gain[None, :], wo=out_weight, gain2=ffn_gain[None, :],
        gate=ffn_gate, up=ffn_up, down=ffn_down, out_grad=out_grad,
    )
    param_shape = (2 * taps_count + 8, max(2 * keys, values))
    gains_shape = (8, max(width, head_gain.shape[0]))
    results = dict(
        output=((length, width), bf16),
        input_grad=((length, width), f32),
        pair_in=((2, width, in_width), bf16),
        pair_out=((2, values, width), bf16),
        pair_ffn=((2, rows, 3 * part, width), bf16),
        params=(param_shape, f32),
        gains=(gains_shape, f32),
    )
    token_block = (cols, length, width)
    vector = (8, length)
    ffn_block = ((rows, 3 * part, width), bf16)
    half_block = ((rows, 2, 3 * part, width // 2), bf16)
    grid_block = ((cols, rows, length, width), bf16)
    row_block = ((rows, length, width), bf16)
    unit_block = ((cols, length, part), bf16)
    scratch = dict(
        xng=(token_block, bf16), og4=grid_block, n24=grid_block,
        xr=((rows, length, width), bf16), w_all=((rows, 2, width // 2, in_width), bf16),
        ss1_recv=((rows,) + vector, f32), ss2_recv=((rows,) + vector, f32),
        lin=((length, in_width), f32), inverse=((heads, length, length), f32),
        mixg=((rows, length, values), bf16),
        d_send=(token_block, f32), d_recv=(token_block, f32),
        resid=((length, width), f32),
        ffn_send=half_block, ffn_all=half_block, wg_send=ffn_block,
        hid=unit_block, gg=unit_block, gu=unit_block,
        t2_send=((cols,) + vector, f32), t2c_recv=((cols,) + vector, f32),
        t2g=((rows,) + vector, f32),
        gi_send=grid_block, gi_recv=grid_block, i_send=row_block, i_recv=row_block,
        go_send=grid_block, go_recv=grid_block, o_send=row_block, o_recv=row_block,
        grad_resid=((length, width), f32), grg=(token_block, bf16),
        k_send=((rows, length, values), bf16), k_recv=((rows, length, values), bf16),
        upstream=((length, values), f32),
        lg=((rows, length, in_width), bf16), t1g=((rows,) + vector, f32),
        m_send=(token_block, bf16), m_recv=(token_block, bf16), t1_recv=((cols,) + vector, f32),
        p_recv=((rows,) + param_shape, f32),
        far_p=((groups,) + param_shape, f32),
        far_g=((groups * cols,) + gains_shape, f32),
    )
    link_count = 20
    semaphores = dict(
        sems=pltpu.SemaphoreType.DMA((link_count, 2, max(rows, cols))),
        far_sems=pltpu.SemaphoreType.DMA((2, 2, groups * cols)),
        dp_sems=pltpu.SemaphoreType.DMA((3, 2)),
        half_sems=pltpu.SemaphoreType.DMA((2, 2, 2, rows, 2)),
        grid_sems=pltpu.SemaphoreType.DMA((4, 2, cols, rows)),
    )
    names = tuple(operands) + tuple(results) + tuple(scratch) + tuple(semaphores)
    features = width * rows
    made = pl.pallas_call(
        functools.partial(block_kernel, (groups, rows, cols, heads, features), names),
        out_shape=tuple(jax.ShapeDtypeStruct(*entry) for entry in results.values()),
        in_specs=[smem] * 4 + [vmem] * (len(operands) - 4),
        out_specs=tuple([vmem] * len(results)),
        scratch_shapes=[pltpu.VMEM(*entry) for entry in scratch.values()]
        + list(semaphores.values()),
        compiler_params=pltpu.CompilerParams(
            collective_id=0, has_side_effects=True, vmem_limit_bytes=58 * 1024 * 1024
        ),
        name="residual_block",
    )(*operands.values())
    made = list(made)
    if groups != 2:
        for place in range(2, 5):
            whole = lax.psum(made[place][0], "dp")
            made[place] = jnp.stack([whole, jnp.zeros_like(whole)])
    finals = (
        block_input, jax.ShapeDtypeStruct((length, width), f32), attn_gain[None, :],
        query_weight, key_weight, value_weight, gate_weight, decay_weight, beta_weight,
        query_conv, key_conv, value_conv, decay_log[None, :], decay_bias[None, :],
        head_gain[None, :], out_weight, ffn_gain[None, :], ffn_gate, ffn_up, ffn_down,
    )
    given = made[2:] + made[:2]
    final = pl.pallas_call(
        functools.partial(finish_kernel, heads, taps_count),
        out_shape=tuple(
            jax.ShapeDtypeStruct(entry.shape, bf16 if place == 0 else f32)
            for place, entry in enumerate(finals)
        ),
        in_specs=[vmem] * len(given),
        out_specs=tuple([vmem] * len(finals)),
        compiler_params=pltpu.CompilerParams(vmem_limit_bytes=40 * 1024 * 1024),
        name="group_sums",
    )(*given)
    final = list(final)
    for place in (2, 12, 13, 14, 16):
        final[place] = final[place][0]
    return tuple(final)


def solution(mesh):
    in_specs = (
        P(("dp", "col"), "row"),
        P("row"),
        P("row", "col"),
        P("row", "col"),
        P("row", "col"),
        P("row", "col"),
        P("row", "col"),
        P("row", "col"),
        P(None, "col"),
        P(None, "col"),
        P(None, "col"),
        P("col"),
        P("col"),
        P(),
        P("col", "row"),
        P("row"),
        P("row", "col"),
        P("row", "col"),
        P("col", "row"),
        P(("dp", "col"), "row"),
        P(),
        P(),
    )
    out_specs = (
        P(("dp", "col"), "row"),
        P(("dp", "col"), "row"),
        P("row"),
        P("row", "col"),
        P("row", "col"),
        P("row", "col"),
        P("row", "col"),
        P("row", "col"),
        P("row", "col"),
        P(None, "col"),
        P(None, "col"),
        P(None, "col"),
        P("col"),
        P("col"),
        P(),
        P("col", "row"),
        P("row"),
        P("row", "col"),
        P("row", "col"),
        P("col", "row"),
    )
    return jax.shard_map(shards, mesh=mesh, in_specs=in_specs, out_specs=out_specs, check_vma=False)
```

```python
import functools
import types

import jax
import jax.numpy as jnp
from jax import lax
from jax.experimental import pallas as pl
from jax.experimental.pallas import tpu as pltpu
from jax.sharding import PartitionSpec as P

epsilon = 1e-06
highest = lax.Precision.HIGHEST


def fp_dot(left, right, left_dim, right_dim):
    return lax.dot_general(
        left,
        right,
        (((left_dim,), (right_dim,)), ((), ())),
        precision=highest,
        preferred_element_type=jnp.float32,
    )


def plain_softplus(values):
    return jnp.maximum(values, 0.0) + jnp.log1p(jnp.exp(-jnp.abs(values)))


@jax.custom_vjp
def smooth_ramp(values):
    return plain_softplus(values)


smooth_ramp.defvjp(
    lambda values: (plain_softplus(values), values),
    lambda values, upstream: (upstream * lax.logistic(values),),
)


@jax.custom_vjp
def apply_inverse(inverse, lower_part, target):
    return fp_dot(inverse, target, 1, 0)


def apply_inverse_forward(inverse, lower_part, target):
    writes = fp_dot(inverse, target, 1, 0)
    return writes, (inverse, writes)


def apply_inverse_backward(saved, upstream):
    inverse, writes = saved
    grad_target = fp_dot(inverse, upstream, 0, 0)
    return (jnp.zeros_like(inverse), -fp_dot(grad_target, writes, 1, 1), grad_target)


apply_inverse.defvjp(apply_inverse_forward, apply_inverse_backward)


def unit_lower_inverse(lower_part, row_index, column_index):
    length = lower_part.shape[0]
    inverse = jnp.where(row_index == column_index, 1.0, 0.0)
    level = 0
    while (1 << level) < length:
        row_block = row_index >> level
        column_block = column_index >> level
        joined = (row_block == column_block + 1) & ((column_block & 1) == 0)
        corner = jnp.where(joined, lower_part, 0.0)
        if level == 0:
            inverse = inverse - corner
        else:
            inverse = inverse - fp_dot(fp_dot(inverse, corner, 1, 0), inverse, 1, 0)
        level += 1
    return inverse


def slot_masks(bounds, length, tap_count):
    row_index = lax.broadcasted_iota(jnp.int32, (length, length), 0)
    column_index = lax.broadcasted_iota(jnp.int32, (length, length), 1)
    token = lax.broadcasted_iota(jnp.int32, (length, 1), 0)
    row_segment = jnp.zeros((length, length), jnp.int32)
    column_segment = jnp.zeros((length, length), jnp.int32)
    inside = jnp.zeros((length, 1), jnp.float32)
    for begin, count in zip(*bounds):
        end = begin + count
        row_segment += jnp.where(row_index >= begin, 1, 0) + jnp.where(row_index >= end, 1, 0)
        column_segment += jnp.where(column_index >= begin, 1, 0)
        column_segment += jnp.where(column_index >= end, 1, 0)
        inside += jnp.where((token >= begin) & (token < end), 1.0, 0.0)
    same = row_segment == column_segment
    shifts = [
        jnp.where(same & (column_index == row_index - offset), 1.0, 0.0)
        for offset in range(1, tap_count)
    ]
    return dict(
        row_index=row_index,
        column_index=column_index,
        shifts=shifts,
        strict=jnp.where(same & (row_index > column_index), 1.0, 0.0),
        within=jnp.where(same & (row_index >= column_index), 1.0, 0.0),
        upto=jnp.where(row_index >= column_index, 1.0, 0.0),
        later=jnp.where(row_index > column_index, 1.0, 0.0),
        inside=inside,
    )


def conv_head(signal, taps, shifts):
    total = taps[-1] * signal
    for offset, shift in enumerate(shifts, 1):
        total = total + taps[len(taps) - 1 - offset] * fp_dot(shift, signal, 1, 0)
    return total * lax.logistic(total)


def unit_rows(values):
    return values * lax.rsqrt(jnp.sum(values * values, axis=1, keepdims=True) + epsilon)


def mixer_head(masks, inverse, bias, linears, taps, rate, norm_gain):
    query_lin, key_lin, value_lin, gate_lin, decay_lin, rate_lin = linears
    differentiated = inverse is not None
    queries = unit_rows(conv_head(query_lin, taps[0], masks["shifts"]))
    queries = queries * queries.shape[1] ** (-0.5)
    keys = unit_rows(conv_head(key_lin, taps[1], masks["shifts"]))
    values = conv_head(value_lin, taps[2], masks["shifts"])
    write_rate = lax.logistic(rate_lin)
    ramp = smooth_ramp if differentiated else plain_softplus
    log_decay = -rate * ramp(decay_lin + bias)
    ratio = jnp.exp(fp_dot(masks["upto"], log_decay * masks["later"], 1, 0))
    lower_part = write_rate * ratio * fp_dot(keys, keys, 1, 1) * masks["strict"]
    target = write_rate * values
    if differentiated:
        writes = apply_inverse(inverse, lower_part, target)
    else:
        inverse = unit_lower_inverse(lower_part, masks["row_index"], masks["column_index"])
        writes = fp_dot(inverse, target, 1, 0)
    heads = fp_dot(ratio * fp_dot(queries, keys, 1, 1) * masks["within"], writes, 1, 0)
    mean_square = jnp.sum(heads * heads, axis=1, keepdims=True) * (1.0 / heads.shape[1])
    normed = heads * lax.rsqrt(mean_square + epsilon) * norm_gain
    gated = normed * (gate_lin * lax.logistic(gate_lin)) * masks["inside"]
    return (gated, inverse)


LANES = 128
MESH = pl.DeviceIdType.MESH


def head_operands(h, heads, lin_ref, conv_refs, log_ref, bias_ref, gain_ref):
    length = lin_ref.shape[0]
    key_size = conv_refs[0].shape[1] // heads
    value_size = conv_refs[2].shape[1] // heads
    widths = (key_size, key_size, value_size, value_size)
    spans = []
    base = 0
    for width in widths:
        spans.append(slice(base + h * width, base + (h + 1) * width))
        base += heads * width
    tail = lin_ref[:, base : base + LANES]
    lane = lax.broadcasted_iota(jnp.int32, tail.shape, 1)
    columns = [
        jnp.sum(jnp.where(lane == place, tail, 0.0), axis=1, keepdims=True)
        for place in (h, heads + h)
    ]
    linears = tuple(lin_ref[:, span] for span in spans) + tuple(columns)
    tap_spans = [slice(h * width, (h + 1) * width) for width in widths[:3]]
    taps = tuple(
        tuple(ref[i : i + 1, span] for i in range(ref.shape[0]))
        for ref, span in zip(conv_refs, tap_spans)
    )
    rate = jnp.exp(jnp.full((length, 1), log_ref[h], jnp.float32))
    bias = jnp.full((length, 1), bias_ref[h], jnp.float32)
    return linears, taps, rate, bias, gain_ref[...], spans, tap_spans, base


def spread_columns(columns):
    shape = (columns[0].shape[0], LANES)
    lane = lax.broadcasted_iota(jnp.int32, shape, 1)
    total = jnp.zeros(shape, jnp.float32)
    for place, column in enumerate(columns):
        total = total + jnp.where(lane == place, column, 0.0)
    return total


def wrap(index, count):
    return lax.rem(index, count)


def dot_nn(left, right):
    return lax.dot_general(
        left, right, (((1,), (0,)), ((), ())), preferred_element_type=jnp.float32
    )


def dot_nt(left, right):
    return lax.dot_general(
        left, right, (((1,), (1,)), ((), ())), preferred_element_type=jnp.float32
    )


def dot_tn(left, right):
    return lax.dot_general(
        left, right, (((0,), (0,)), ((), ())), preferred_element_type=jnp.float32
    )


def diagonal(length):
    row = lax.broadcasted_iota(jnp.int32, (length, length), 0)
    column = lax.broadcasted_iota(jnp.int32, (length, length), 1)
    return row == column


def as_row(column):
    length = column.shape[0]
    return jnp.sum(jnp.where(diagonal(length), column, 0.0), axis=0, keepdims=True)


def as_column(row):
    length = row.shape[1]
    return jnp.sum(jnp.where(diagonal(length), row, 0.0), axis=1, keepdims=True)


class Link:
    def __init__(self, axis, count, me, landing, sems, place):
        self.axis, self.count, self.me = axis, count, me
        self.landing, self.sems, self.place = landing, sems, place
        self.source = None

    def copy(self, source, target, slot):
        return pltpu.make_async_remote_copy(
            src_ref=source,
            dst_ref=self.landing.at[slot],
            send_sem=self.sems.at[self.place, 0, target],
            recv_sem=self.sems.at[self.place, 1, slot],
            device_id={self.axis: target},
            device_id_type=MESH,
        )

    def send(self, source, target):
        self.copy(source, target, self.me).start()

    def spread(self):
        source = self.landing.at[self.me]
        for k in range(1, self.count):
            self.send(source, wrap(self.me + k, self.count))

    def arrive(self, slot):
        self.copy(self.landing.at[slot], slot, slot).wait_recv()

    def drain(self):
        for k in range(1, self.count):
            target = wrap(self.me + k, self.count)
            source = self.landing.at[self.me] if self.source is None else self.source.at[target]
            self.copy(source, target, self.me).wait_send()


def block_kernel(sizes, names, *flat):
    ref = types.SimpleNamespace(**dict(zip(names, flat)))
    groups, rows, cols, heads, features = sizes
    d, r, c = lax.axis_index("dp"), lax.axis_index("row"), lax.axis_index("col")
    sems, far_sems, dp_sems = ref.sems, ref.far_sems, ref.dp_sems
    grid_sems, half_sems = ref.grid_sems, ref.half_sems
    spread_count = groups * cols
    mine = d * cols + c

    barrier = pltpu.get_barrier_semaphore()
    for k in range(1, rows):
        pl.semaphore_signal(
            barrier, inc=1, device_id={"row": wrap(r + k, rows)}, device_id_type=MESH
        )

    def greet(k, carry):
        other = wrap(mine + k, spread_count)
        pl.semaphore_signal(
            barrier,
            inc=1,
            device_id={"dp": other // cols, "col": wrap(other, cols)},
            device_id_type=MESH,
        )
        return carry

    lax.fori_loop(1, spread_count, greet, 0)
    pl.semaphore_wait(barrier, rows - 1 + spread_count - 1)

    links = []

    def link_row(landing):
        links.append(Link("row", rows, r, landing, sems, len(links)))
        return links[-1]

    def link_col(landing):
        links.append(Link("col", cols, c, landing, sems, len(links)))
        return links[-1]

    x_link, og_link = link_col(ref.xng), link_row(ref.og4.at[c])
    b_link, ss1_link = link_row(ref.xr), link_row(ref.ss1_recv)
    mix_link, d_link = link_row(ref.mixg), link_col(ref.d_recv)
    n2_link, ss2_link = link_row(ref.n24.at[c]), link_row(ref.ss2_recv)
    wg_links = [link_row(ref.ffn_sum.at[half]) for half in ((d,) if groups == 2 else (0, 1))]
    i_link, o_link = link_row(ref.i_recv), link_row(ref.o_recv)
    t2c_link, t2_link = link_col(ref.t2c_recv), link_row(ref.t2g)
    gr_link, k_link = link_col(ref.grg), link_row(ref.k_recv)
    l_links = [link_row(ref.lg.at[h]) for h in range(heads)]
    lt_link, t1_link = link_row(ref.lt), link_row(ref.t1g)
    m_link, t1c_link = link_col(ref.m_recv), link_col(ref.t1_recv)
    p_link = link_row(ref.p_recv)

    def grid_copy(place, source, landing, target, slot, j):
        return pltpu.make_async_remote_copy(
            src_ref=source,
            dst_ref=landing.at[slot, j],
            send_sem=grid_sems.at[place, 0, target, j],
            recv_sem=grid_sems.at[place, 1, slot, j],
            device_id={"col": target},
            device_id_type=MESH,
        )

    halves = (d,) if groups == 2 else (0, 1)
    half_sent = []

    def half_copy(place, hop, source, landing, target, slot, half, peer):
        return pltpu.make_async_remote_copy(
            src_ref=source,
            dst_ref=landing.at[slot, half],
            send_sem=half_sems.at[place, hop, 0, target, half],
            recv_sem=half_sems.at[place, hop, 1, slot, half],
            device_id=peer,
            device_id_type=MESH,
        )

    def weights_out(place, source, landing):
        for k in range(1, rows):
            t = wrap(r + k, rows)
            for half in halves:
                copy = half_copy(place, 0, source(t, half), landing, t, r, half, {"row": t})
                copy.start()
                half_sent.append(copy)

    def weights_across(place, landing):
        for k in range(1, rows):
            j = wrap(r + k, rows)
            for half in halves:
                here = landing.at[j, half]
                half_copy(place, 0, here, landing, j, j, half, {"row": j}).wait_recv()
                if groups == 2:
                    copy = half_copy(place, 1, here, landing, j, j, half, {"dp": 1 - d})
                    copy.start()
                    half_sent.append(copy)

    def weights_in(place, landing):
        if groups == 2:
            for k in range(1, rows):
                j = wrap(r + k, rows)
                here = landing.at[j, 1 - d]
                half_copy(place, 1, here, landing, j, j, 1 - d, {"dp": 1 - d}).wait_recv()

    grid_sent = []

    def grid_send(place, source, landing, target, j):
        copy = grid_copy(place, source, landing, target, c, j)
        copy.start()
        grid_sent.append(copy)

    def grid_arrive(place, landing, slot, j):
        grid_copy(place, landing.at[slot, j], landing, slot, slot, j).wait_recv()

    def onward(row_link, place, blocks):
        for k in range(rows):
            j = gathered(row_link, k)
            for step in range(1, cols):
                grid_send(place, blocks.at[c, j], blocks, wrap(c + step, cols), j)

    def gathered(link_used, k):
        slot = wrap(link_used.me + k, link_used.count)
        if k:
            link_used.arrive(slot)
        return slot

    def pass_on(link_used, send, target):
        link_used.source = send

        @pl.when(target != link_used.me)
        def _():
            link_used.send(send.at[target], target)

    def total(link_used, send):
        running = send[link_used.me].astype(jnp.float32)
        for k in range(1, link_used.count):
            slot = wrap(link_used.me + k, link_used.count)
            link_used.arrive(slot)
            running = running + link_used.landing[slot].astype(jnp.float32)
        return running

    bf16 = jnp.bfloat16

    ref.og4[c, r] = ref.out_grad[...]

    def send_squares(link_used, values):
        sums = link_used.landing
        sums[r, 0:1, :] = as_row(jnp.sum(values * values, axis=1, keepdims=True))
        link_used.spread()

    def row_scale(link_used):
        sums = link_used.landing
        for k in range(1, rows):
            link_used.arrive(wrap(r + k, rows))
        running = sums[0, 0:1, :]
        for j in range(1, rows):
            running = running + sums[j, 0:1, :]
        return lax.rsqrt(as_column(running) * (1.0 / features) + epsilon)

    gain1 = ref.gain1[...]
    gain2 = ref.gain2[...]
    inputs = ref.x[...].astype(jnp.float32)
    send_squares(ss1_link, inputs)
    in_refs = (ref.wq, ref.wk, ref.wv, ref.wg, ref.wt)
    in_spans = []
    base = 0
    depth = ref.w_all.shape[2]
    for weight in in_refs:
        width = weight.shape[1]
        in_spans.append(slice(base, base + width))
        base += width
        for half in range(2):
            ref.w_all[r, half, :, in_spans[-1]] = weight[half * depth : (half + 1) * depth, :]
    scale1 = row_scale(ss1_link)
    weights_out(0, lambda t, half: ref.w_all.at[r, half], ref.w_all)
    ref.xng[c] = (inputs * scale1 * gain1).astype(bf16)
    x_link.spread()
    for k in range(cols):
        t = gathered(x_link, k)
        pass_on(b_link, ref.xng, t)
    og_link.spread()

    width, hidden = ref.gate.shape
    part = hidden // rows
    identity = jnp.where(diagonal(width), 1.0, 0.0).astype(bf16)
    for place, weight in enumerate((ref.gate, ref.up)):
        turned = dot_tn(weight[...], identity)
        for j in range(rows):
            for half in range(2):
                ref.ffn_send[j, half, place * part : (place + 1) * part, :] = turned[
                    j * part : (j + 1) * part, half * depth : (half + 1) * depth
                ].astype(bf16)
    for j in range(rows):
        for half in range(2):
            ref.ffn_send[j, half, 2 * part : 3 * part, :] = ref.down[
                j * part : (j + 1) * part, half * depth : (half + 1) * depth
            ]
    weights_out(1, lambda t, half: ref.ffn_send.at[t, half], ref.ffn_all)
    ref.ffn_all[r] = ref.ffn_send[r]

    def share(j, span):
        return jnp.concatenate([ref.ffn_all[j, half, span, :] for half in range(2)], axis=1)


    def row_total(link_used, send):
        running = send[link_used.me, 0:1, :]
        for k in range(1, link_used.count):
            slot = wrap(link_used.me + k, link_used.count)
            link_used.arrive(slot)
            running = running + link_used.landing[slot, 0:1, :]
        return running

    ref.xr[r] = ref.xng[r]
    weights_across(0, ref.w_all)
    for k in range(1, rows):
        b_link.arrive(wrap(r + k, rows))
    weights_in(0, ref.w_all)
    for span in in_spans:
        ref.lin[:, span] = sum(
            dot_nn(ref.xr[j], ref.w_all[j, :, :, span].reshape(2 * depth, span.stop - span.start))
            for j in range(rows)
        )
    lin_ref = ref.lin
    length = lin_ref.shape[0]
    conv_refs = (ref.qc, ref.kc, ref.vc)
    slot_index = d * cols + r
    starts = [ref.starts[slot_index, i] for i in range(ref.starts.shape[1])]
    counts = [ref.counts[slot_index, i] for i in range(ref.counts.shape[1])]
    masks = slot_masks((starts, counts), length, conv_refs[0].shape[0])
    for h in range(heads):
        linears, taps, rate, bias, gain, _, tap_spans, _ = head_operands(
            h, heads, lin_ref, conv_refs, ref.log, ref.bias, ref.norm_gain
        )
        gated, inverse = mixer_head(masks, None, bias, linears, taps, rate, gain)
        ref.mixg[r, :, tap_spans[2]] = gated.astype(bf16)
        ref.inverse[h] = inverse
    mix_link.spread()
    for k in range(rows):
        t = gathered(mix_link, k)
        ref.d_send[t] = dot_nn(ref.mixg[t], ref.wo[...])
        pass_on(d_link, ref.d_send, t)
    onward(og_link, 0, ref.og4)
    weights_across(1, ref.ffn_all)
    resid = inputs + total(d_link, ref.d_send)
    ref.resid[...] = resid
    send_squares(ss2_link, resid)
    scale2 = row_scale(ss2_link)
    ref.n24[c, r] = (resid * scale2 * gain2).astype(bf16)
    n2_link.spread()
    onward(n2_link, 1, ref.n24)

    weights_in(1, ref.ffn_all)
    token = lax.broadcasted_iota(jnp.int32, (length, 1), 0)
    places = [slice(i * part, (i + 1) * part) for i in range(3)]
    for k in range(cols):
        t = wrap(c + k, cols)
        if k:
            for j in range(rows):
                grid_arrive(0, ref.og4, t, j)
            for j in range(rows):
                grid_arrive(1, ref.n24, t, j)
        gate_part, up_part, grad_hidden = (
            sum(dot_nt(tokens[t, j], share(j, span)) for j in range(rows))
            for tokens, span in zip((ref.n24, ref.n24, ref.og4), places)
        )
        inside = jnp.zeros((length, 1), jnp.float32)
        for i in range(ref.starts.shape[1]):
            begin = ref.starts[d * cols + t, i]
            end = begin + ref.counts[d * cols + t, i]
            inside += jnp.where((token >= begin) & (token < end), 1.0, 0.0)
        grad_hidden = grad_hidden * inside
        sigmoid = lax.logistic(gate_part)
        ref.hid[t] = (gate_part * sigmoid * up_part * inside).astype(bf16)
        grad_gate = grad_hidden * up_part * sigmoid * (1.0 + gate_part * (1.0 - sigmoid))
        grad_up = grad_hidden * gate_part * sigmoid
        ref.gg[t] = grad_gate.astype(bf16)
        ref.gu[t] = grad_up.astype(bf16)
        inner_sum = jnp.sum(grad_gate * gate_part + grad_up * up_part, axis=1, keepdims=True)
        ref.t2_send[t, 0:1, :] = as_row(inner_sum)
        pass_on(t2c_link, ref.t2_send, t)

    def all_tokens(source):
        block = source[...]
        return block.reshape(block.shape[0] * block.shape[1], block.shape[2])

    def feature_sums(place, send, landing, grads):
        for k in range(1, rows + 1):
            j = wrap(r + k, rows)
            terms = sum(dot_nn(grad, share(j, span)) for grad, span in grads)
            for t in range(cols):
                send[t, j] = terms[t * length : (t + 1) * length].astype(bf16)
            for step in range(1, cols):
                t = wrap(c + step, cols)
                grid_send(place, send.at[t, j], landing, t, j)

    def across_rows(place, send, landing, row_link, row_send):
        for k in range(1, rows + 1):
            j = wrap(r + k, rows)
            running = send[c, j].astype(jnp.float32)
            for step in range(1, cols):
                t = wrap(c + step, cols)
                grid_arrive(place, landing, t, j)
                running = running + landing[t, j].astype(jnp.float32)
            row_send[j] = running.astype(bf16)
            pass_on(row_link, row_send, j)

    feature_sums(
        2, ref.gi_send, ref.gi_recv,
        ((all_tokens(ref.gg), places[0]), (all_tokens(ref.gu), places[1])),
    )
    ref.t2g[r, 0:1, :] = row_total(t2c_link, ref.t2_send)
    t2_link.spread()
    across_rows(2, ref.gi_send, ref.gi_recv, i_link, ref.i_send)

    dp_copies = []

    def trade(source, landing, part):
        if groups == 2:
            copy = pltpu.make_async_remote_copy(
                src_ref=source,
                dst_ref=landing,
                send_sem=dp_sems.at[part, 0],
                recv_sem=dp_sems.at[part, 1],
                device_id={"dp": 1 - d},
                device_id_type=MESH,
            )
            copy.start()
            dp_copies.append(copy)
            return copy

    grad_second = total(i_link, ref.i_send) * scale2
    t2 = as_column(row_total(t2_link, ref.t2g)) * scale2 * scale2 * (1.0 / features)
    resid = ref.resid[...]
    grad_resid = ref.out_grad[...].astype(jnp.float32) + grad_second * gain2 - resid * t2
    ref.grad_resid[...] = grad_resid
    ref.grg[c] = grad_resid.astype(bf16)
    gr_link.spread()
    ffn_gain_part = jnp.sum(grad_second * resid, axis=0, keepdims=True)

    for k in range(cols):
        t = gathered(gr_link, k)
        ref.k_send[t] = dot_nt(ref.grg[t], ref.wo[...]).astype(bf16)
        pass_on(k_link, ref.k_send, t)
    sides = ((ref.gg, ref.n24), (ref.gu, ref.n24), (ref.hid, ref.og4))
    lefts = [all_tokens(left) for left, _ in sides]
    for j in range(rows):
        for span, left, (_, right) in zip(places, lefts, sides):
            tokens = right[:, j].reshape(cols * length, width)
            grads = dot_tn(left, tokens).astype(bf16)
            for half in range(2):
                ref.wg_send[half, j, span, :] = grads[:, half * depth : (half + 1) * depth]
    if groups == 2:
        wg_trade = trade(ref.wg_send.at[1 - d], ref.wg_recv, 1)
    feature_sums(3, ref.go_send, ref.go_recv, ((all_tokens(ref.hid), places[2]),))
    ref.pair_out[0] = dot_tn(all_tokens(ref.mixg), all_tokens(ref.grg)).astype(bf16)
    trade(ref.pair_out.at[0], ref.pair_out.at[1], 0)
    across_rows(3, ref.go_send, ref.go_recv, o_link, ref.o_send)

    ref.upstream[...] = total(k_link, ref.k_send)
    if groups == 2:
        wg_trade.wait_recv()
        dp_copies.remove(wg_trade)
        for k in range(1, rows + 1):
            j = wrap(r + k, rows)
            both = ref.wg_send[d, j].astype(jnp.float32) + ref.wg_recv[j].astype(jnp.float32)
            ref.wg_sum[j] = both.astype(bf16)
            pass_on(wg_links[0], ref.wg_sum, j)
        ref.ffn_sum[d, r] = ref.wg_sum[r]
    else:
        for half in range(2):
            for k in range(1, rows):
                pass_on(wg_links[half], ref.wg_send.at[half], wrap(r + k, rows))
            ref.ffn_sum[half, r] = ref.wg_send[half, r]
    masks = slot_masks((starts, counts), length, conv_refs[0].shape[0])
    decay_columns, rate_columns, log_columns = [], [], []
    gain_total = jnp.zeros(ref.norm_gain.shape, jnp.float32)
    inner_sum = jnp.zeros((length, 1), jnp.float32)
    params = ref.p_recv
    params[r] = jnp.zeros(params.shape[1:], jnp.float32)
    taps_count = conv_refs[0].shape[0]
    key_width = conv_refs[0].shape[1]
    head_spans, head_weights = [], [[] for h in range(heads)]
    base = 0
    for weight in in_refs[:4]:
        size = weight.shape[1] // heads
        head_spans.append(slice(base, base + size))
        base += size
        for h in range(heads):
            head_weights[h].append((weight, slice(h * size, (h + 1) * size)))
    for h in range(heads):
        linears, taps, rate, bias, gain, spans, tap_spans, tail_base = head_operands(
            h, heads, lin_ref, conv_refs, ref.log, ref.bias, ref.norm_gain
        )
        inverse = ref.inverse[h]

        def piece(linear_set, tap_set, rate_set, gain_set):
            return mixer_head(masks, inverse, bias, linear_set, tap_set, rate_set, gain_set)[0]

        _, back = jax.vjp(piece, linears, taps, rate, gain)
        grad_linears, grad_taps, grad_rate, grad_gain = back(ref.upstream[:, tap_spans[2]])
        for span, grad in zip(head_spans, grad_linears):
            ref.lg[h, r, :, span] = grad.astype(bf16)
        if h + 1 < heads:
            l_links[h].spread()
        for grad, linear in zip(grad_linears, linears):
            inner_sum = inner_sum + jnp.sum(grad * linear, axis=1, keepdims=True)
        places = ((taps_count, 0), (taps_count, key_width), (0, 0))
        for (top, left), span, grads in zip(places, tap_spans, grad_taps):
            for i, grad in enumerate(grads):
                params[r, top + i : top + i + 1, left + span.start : left + span.stop] = grad
        gain_total = gain_total + grad_gain
        decay_columns.append(grad_linears[4])
        rate_columns.append(grad_linears[5])
        log_columns.append(grad_rate * rate)
    tails = spread_columns(decay_columns + rate_columns)
    ref.lt[r] = tails.astype(bf16)
    lt_link.spread()
    ref.t1g[r, 0:1, :] = as_row(inner_sum)
    t1_link.spread()
    value_size = gain_total.shape[1]
    params[r, 2 * taps_count : 2 * taps_count + 1, 0:value_size] = gain_total
    params[r, 2 * taps_count + 1 : 2 * taps_count + 2, 0:LANES] = jnp.sum(
        spread_columns(log_columns + decay_columns), axis=0, keepdims=True
    )
    p_link.spread()
    l_links[heads - 1].spread()
    ref.output[...] = (ref.resid[...] + total(o_link, ref.o_send)).astype(bf16)
    for used in wg_links:
        for k in range(1, rows):
            used.arrive(wrap(r + k, rows))
    trade(ref.ffn_sum.at[d], ref.ffn_sum.at[d], 2)

    first_all = all_tokens(ref.xng)

    def head_grads(h):
        ref.pair_in[0, h] = dot_tn(first_all, all_tokens(ref.lg.at[h])).astype(bf16)
        trade(ref.pair_in.at[0, h], ref.pair_in.at[1, h], 4 + h)

    for h in range(heads - 1):
        for k in range(rows):
            gathered(l_links[h], k)
        head_grads(h)
    for k in range(rows):
        t = gathered(t1_link, k)
        pass_on(t1c_link, ref.t1g, t)
        gathered(lt_link, k)
        gathered(l_links[heads - 1], k)
        terms = dot_nt(ref.lt[t], ref.wt[...])
        for h in range(heads):
            for span, (weight, columns) in zip(head_spans, head_weights[h]):
                terms = terms + dot_nt(ref.lg[h, t, :, span], weight[:, columns])
        ref.m_send[t] = terms.astype(bf16)
        pass_on(m_link, ref.m_send, t)
    ref.pair_tail[0] = dot_tn(first_all, all_tokens(ref.lt)).astype(bf16)
    trade(ref.pair_tail.at[0], ref.pair_tail.at[1], 3)
    head_grads(heads - 1)

    for k in range(1, rows):
        p_link.arrive(wrap(r + k, rows))
    summed = params[0]
    for j in range(1, rows):
        summed = summed + params[j]
    far_p, far_g = ref.far_p, ref.far_g
    far_p[d] = summed

    def far_copy(landing, place, slot, target, peer):
        return pltpu.make_async_remote_copy(
            src_ref=landing.at[slot],
            dst_ref=landing.at[slot],
            send_sem=far_sems.at[place, 0, target],
            recv_sem=far_sems.at[place, 1, slot],
            device_id=peer,
            device_id_type=MESH,
        )

    def dp_peers(act):
        def step(k, carry):
            other = wrap(d + k, groups)
            act(other, {"dp": other})
            return carry

        lax.fori_loop(1, groups, step, 0)

    def far_peers(act):
        def step(k, carry):
            other = wrap(mine + k, spread_count)
            act(other, {"dp": other // cols, "col": wrap(other, cols)})
            return carry

        lax.fori_loop(1, spread_count, step, 0)

    dp_peers(lambda other, peer: far_copy(far_p, 0, d, other, peer).start())

    grad_first = total(m_link, ref.m_send) * scale1
    t1 = as_column(row_total(t1c_link, ref.t1g)) * scale1 * scale1 * (1.0 / features)
    ref.input_grad[...] = ref.grad_resid[...] + grad_first * gain1 - inputs * t1
    far_g[mine] = jnp.zeros(far_g.shape[1:], jnp.float32)
    far_g[mine, 0:1, :] = jnp.sum(grad_first * inputs, axis=0, keepdims=True)
    far_g[mine, 1:2, :] = ffn_gain_part
    far_g[mine, 2:3, 0:value_size] = summed[2 * taps_count : 2 * taps_count + 1, 0:value_size]
    far_peers(lambda other, peer: far_copy(far_g, 1, mine, other, peer).start())
    dp_peers(lambda other, peer: far_copy(far_p, 0, other, other, peer).wait_recv())
    far_peers(lambda other, peer: far_copy(far_g, 1, other, other, peer).wait_recv())
    ref.params[...] = lax.fori_loop(1, groups, lambda j, acc: acc + far_p[j], far_p[0])
    ref.gains[...] = lax.fori_loop(1, spread_count, lambda j, acc: acc + far_g[j], far_g[0])
    for copy in dp_copies:
        copy.wait_recv()

    dp_peers(lambda other, peer: far_copy(far_p, 0, d, other, peer).wait_send())
    far_peers(lambda other, peer: far_copy(far_g, 1, mine, other, peer).wait_send())
    for copy in dp_copies:
        copy.wait_send()
    if groups == 2:
        wg_trade.wait_send()
    for copy in grid_sent + half_sent:
        copy.wait_send()
    for used in links:
        used.drain()


def finish_kernel(heads, taps_count, *refs):
    (pair_in, pair_tail, pair_out, ffn_sum, params, gains, out_in, grad_in) = refs[:8]
    (output, input_grad, attn, gq, gk, gv, gg, gd, gb, cq, ck, cv, dl, db, hg, go, fg, gate, up, down) = refs[8:]

    def both(pair, *index):
        return pair[(0,) + index].astype(jnp.float32) + pair[(1,) + index].astype(jnp.float32)

    output[...] = out_in[...]
    input_grad[...] = grad_in[...]
    attn[...] = gains[0:1, :]
    fg[...] = gains[1:2, :]
    hg[...] = gains[2:3, 0 : hg.shape[1]]
    base = 0
    every = slice(None)
    for ref in (gq, gk, gv, gg):
        size = ref.shape[1] // heads
        for h in range(heads):
            ref[:, h * size : (h + 1) * size] = both(pair_in, h, every, slice(base, base + size))
        base += size
    tail = both(pair_tail)
    gd[...] = tail[:, 0:heads]
    gb[...] = tail[:, heads : 2 * heads]
    key_width = cq.shape[1]
    cv[...] = params[0:taps_count, :]
    cq[...] = params[taps_count : 2 * taps_count, 0:key_width]
    ck[...] = params[taps_count : 2 * taps_count, key_width : 2 * key_width]
    dl[...] = params[2 * taps_count + 1 : 2 * taps_count + 2, 0:heads]
    db[...] = params[2 * taps_count + 1 : 2 * taps_count + 2, heads : 2 * heads]
    go[...] = both(pair_out)
    rows, part = ffn_sum.shape[1], ffn_sum.shape[2] // 3
    identity = jnp.where(diagonal(gate.shape[0]), 1.0, 0.0).astype(jnp.bfloat16)

    def units(j, place):
        span = slice(place * part, (place + 1) * part)
        return jnp.concatenate([ffn_sum[half, j, span, :] for half in range(2)], axis=1)

    for place, ref in enumerate((gate, up)):
        whole = jnp.concatenate([units(j, place) for j in range(rows)], axis=0)
        ref[...] = dot_nt(identity, whole)
    for j in range(rows):
        down[j * part : (j + 1) * part, :] = units(j, 2).astype(jnp.float32)


def shards(
    block_input,
    attn_gain,
    query_weight,
    key_weight,
    value_weight,
    gate_weight,
    decay_weight,
    beta_weight,
    query_conv,
    key_conv,
    value_conv,
    decay_log,
    decay_bias,
    head_gain,
    out_weight,
    ffn_gain,
    ffn_gate,
    ffn_up,
    ffn_down,
    out_grad,
    seq_starts,
    seq_lengths,
):
    groups, rows, cols = (lax.axis_size(name) for name in ("dp", "row", "col"))
    length, width = block_input.shape
    heads = decay_log.shape[0]
    taps_count = query_conv.shape[0]
    keys, values = query_weight.shape[1], value_weight.shape[1]
    hidden = ffn_gate.shape[1]
    part = hidden // rows
    tail_weight = jnp.concatenate([decay_weight, beta_weight], axis=1)
    tail_weight = jnp.pad(tail_weight, ((0, 0), (0, LANES - tail_weight.shape[1])))
    in_width = 2 * keys + 2 * values + LANES
    head_width = 2 * (keys + values) // heads
    bf16, f32 = jnp.bfloat16, jnp.float32
    smem = pl.BlockSpec(memory_space=pltpu.SMEM)
    vmem = pl.BlockSpec(memory_space=pltpu.VMEM)
    operands = dict(
        starts=seq_starts, counts=seq_lengths, log=decay_log, bias=decay_bias,
        x=block_input, gain1=attn_gain[None, :], wq=query_weight, wk=key_weight,
        wv=value_weight, wg=gate_weight, wt=tail_weight, qc=query_conv, kc=key_conv,
        vc=value_conv, norm_gain=head_gain[None, :], wo=out_weight, gain2=ffn_gain[None, :],
        gate=ffn_gate, up=ffn_up, down=ffn_down, out_grad=out_grad,
    )
    param_shape = (2 * taps_count + 8, max(2 * keys, values))
    gains_shape = (8, max(width, head_gain.shape[0]))
    results = dict(
        output=((length, width), bf16),
        input_grad=((length, width), f32),
        pair_in=((2, heads, width, head_width), bf16),
        pair_tail=((2, width, LANES), bf16),
        pair_out=((2, values, width), bf16),
        ffn_sum=((2, rows, 3 * part, width // 2), bf16),
        params=(param_shape, f32),
        gains=(gains_shape, f32),
    )
    token_block = (cols, length, width)
    vector = (8, length)
    side_block = (rows, 3 * part, width // 2)
    half_block = ((rows, 2, 3 * part, width // 2), bf16)
    grid_block = ((cols, rows, length, width), bf16)
    row_block = ((rows, length, width), bf16)
    unit_block = ((cols, length, part), bf16)
    scratch = dict(
        xng=(token_block, bf16), og4=grid_block, n24=grid_block,
        xr=((rows, length, width), bf16), w_all=((rows, 2, width // 2, in_width), bf16),
        ss1_recv=((rows,) + vector, f32), ss2_recv=((rows,) + vector, f32),
        lin=((length, in_width), f32), inverse=((heads, length, length), f32),
        mixg=((rows, length, values), bf16),
        d_send=(token_block, f32), d_recv=(token_block, f32),
        resid=((length, width), f32),
        ffn_send=half_block, ffn_all=half_block,
        wg_send=((2,) + side_block, bf16), wg_recv=(side_block, bf16), wg_sum=(side_block, bf16),
        hid=unit_block, gg=unit_block, gu=unit_block,
        t2_send=((cols,) + vector, f32), t2c_recv=((cols,) + vector, f32),
        t2g=((rows,) + vector, f32),
        gi_send=grid_block, gi_recv=grid_block, i_send=row_block, i_recv=row_block,
        go_send=grid_block, go_recv=grid_block, o_send=row_block, o_recv=row_block,
        grad_resid=((length, width), f32), grg=(token_block, bf16),
        k_send=((rows, length, values), bf16), k_recv=((rows, length, values), bf16),
        upstream=((length, values), f32),
        lg=((heads, rows, length, head_width), bf16), lt=((rows, length, LANES), bf16), t1g=((rows,) + vector, f32),
        m_send=(token_block, bf16), m_recv=(token_block, bf16), t1_recv=((cols,) + vector, f32),
        p_recv=((rows,) + param_shape, f32),
        far_p=((groups,) + param_shape, f32),
        far_g=((groups * cols,) + gains_shape, f32),
    )
    link_count = 20 + heads + 1
    semaphores = dict(
        sems=pltpu.SemaphoreType.DMA((link_count, 2, max(rows, cols))),
        far_sems=pltpu.SemaphoreType.DMA((2, 2, groups * cols)),
        dp_sems=pltpu.SemaphoreType.DMA((4 + heads, 2)),
        half_sems=pltpu.SemaphoreType.DMA((2, 2, 2, rows, 2)),
        grid_sems=pltpu.SemaphoreType.DMA((4, 2, cols, rows)),
    )
    names = tuple(operands) + tuple(results) + tuple(scratch) + tuple(semaphores)
    features = width * rows
    made = pl.pallas_call(
        functools.partial(block_kernel, (groups, rows, cols, heads, features), names),
        out_shape=tuple(jax.ShapeDtypeStruct(*entry) for entry in results.values()),
        in_specs=[smem] * 4 + [vmem] * (len(operands) - 4),
        out_specs=tuple([vmem] * len(results)),
        scratch_shapes=[pltpu.VMEM(*entry) for entry in scratch.values()]
        + list(semaphores.values()),
        compiler_params=pltpu.CompilerParams(
            collective_id=0, has_side_effects=True, vmem_limit_bytes=58 * 1024 * 1024
        ),
        name="residual_block",
    )(*operands.values())
    made = list(made)
    if groups != 2:
        for place in range(2, 5):
            whole = lax.psum(made[place][0], "dp")
            made[place] = jnp.stack([whole, jnp.zeros_like(whole)])
        made[5] = lax.psum(made[5], "dp")
    finals = (
        block_input, jax.ShapeDtypeStruct((length, width), f32), attn_gain[None, :],
        query_weight, key_weight, value_weight, gate_weight, decay_weight, beta_weight,
        query_conv, key_conv, value_conv, decay_log[None, :], decay_bias[None, :],
        head_gain[None, :], out_weight, ffn_gain[None, :], ffn_gate, ffn_up, ffn_down,
    )
    given = made[2:] + made[:2]
    final = pl.pallas_call(
        functools.partial(finish_kernel, heads, taps_count),
        out_shape=tuple(
            jax.ShapeDtypeStruct(entry.shape, bf16 if place == 0 else f32)
            for place, entry in enumerate(finals)
        ),
        in_specs=[vmem] * len(given),
        out_specs=tuple([vmem] * len(finals)),
        compiler_params=pltpu.CompilerParams(vmem_limit_bytes=40 * 1024 * 1024),
        name="group_sums",
    )(*given)
    final = list(final)
    for place in (2, 12, 13, 14, 16):
        final[place] = final[place][0]
    return tuple(final)


def solution(mesh):
    in_specs = (
        P(("dp", "col"), "row"),
        P("row"),
        P("row", "col"),
        P("row", "col"),
        P("row", "col"),
        P("row", "col"),
        P("row", "col"),
        P("row", "col"),
        P(None, "col"),
        P(None, "col"),
        P(None, "col"),
        P("col"),
        P("col"),
        P(),
        P("col", "row"),
        P("row"),
        P("row", "col"),
        P("row", "col"),
        P("col", "row"),
        P(("dp", "col"), "row"),
        P(),
        P(),
    )
    out_specs = (
        P(("dp", "col"), "row"),
        P(("dp", "col"), "row"),
        P("row"),
        P("row", "col"),
        P("row", "col"),
        P("row", "col"),
        P("row", "col"),
        P("row", "col"),
        P("row", "col"),
        P(None, "col"),
        P(None, "col"),
        P(None, "col"),
        P("col"),
        P("col"),
        P(),
        P("col", "row"),
        P("row"),
        P("row", "col"),
        P("row", "col"),
        P("col", "row"),
    )
    return jax.shard_map(shards, mesh=mesh, in_specs=in_specs, out_specs=out_specs, check_vma=False)
```

```python
import functools
import types

import jax
import jax.numpy as jnp
from jax import lax
from jax.experimental import pallas as pl
from jax.experimental.pallas import tpu as pltpu
from jax.sharding import PartitionSpec as P

epsilon = 1e-06
highest = lax.Precision.HIGHEST


def fp_dot(left, right, left_dim, right_dim):
    return lax.dot_general(
        left,
        right,
        (((left_dim,), (right_dim,)), ((), ())),
        precision=highest,
        preferred_element_type=jnp.float32,
    )


def plain_softplus(values):
    return jnp.maximum(values, 0.0) + jnp.log1p(jnp.exp(-jnp.abs(values)))


@jax.custom_vjp
def smooth_ramp(values):
    return plain_softplus(values)


smooth_ramp.defvjp(
    lambda values: (plain_softplus(values), values),
    lambda values, upstream: (upstream * lax.logistic(values),),
)


@jax.custom_vjp
def apply_inverse(inverse, lower_part, target):
    return fp_dot(inverse, target, 1, 0)


def apply_inverse_forward(inverse, lower_part, target):
    writes = fp_dot(inverse, target, 1, 0)
    return writes, (inverse, writes)


def apply_inverse_backward(saved, upstream):
    inverse, writes = saved
    grad_target = fp_dot(inverse, upstream, 0, 0)
    return (jnp.zeros_like(inverse), -fp_dot(grad_target, writes, 1, 1), grad_target)


apply_inverse.defvjp(apply_inverse_forward, apply_inverse_backward)


def unit_lower_inverse(lower_part, row_index, column_index):
    length = lower_part.shape[0]
    inverse = jnp.where(row_index == column_index, 1.0, 0.0)
    level = 0
    while (1 << level) < length:
        row_block = row_index >> level
        column_block = column_index >> level
        joined = (row_block == column_block + 1) & ((column_block & 1) == 0)
        corner = jnp.where(joined, lower_part, 0.0)
        if level == 0:
            inverse = inverse - corner
        else:
            inverse = inverse - fp_dot(fp_dot(inverse, corner, 1, 0), inverse, 1, 0)
        level += 1
    return inverse


def slot_masks(bounds, length, tap_count):
    row_index = lax.broadcasted_iota(jnp.int32, (length, length), 0)
    column_index = lax.broadcasted_iota(jnp.int32, (length, length), 1)
    token = lax.broadcasted_iota(jnp.int32, (length, 1), 0)
    row_segment = jnp.zeros((length, length), jnp.int32)
    column_segment = jnp.zeros((length, length), jnp.int32)
    inside = jnp.zeros((length, 1), jnp.float32)
    for begin, count in zip(*bounds):
        end = begin + count
        row_segment += jnp.where(row_index >= begin, 1, 0) + jnp.where(row_index >= end, 1, 0)
        column_segment += jnp.where(column_index >= begin, 1, 0)
        column_segment += jnp.where(column_index >= end, 1, 0)
        inside += jnp.where((token >= begin) & (token < end), 1.0, 0.0)
    same = row_segment == column_segment
    shifts = [
        jnp.where(same & (column_index == row_index - offset), 1.0, 0.0)
        for offset in range(1, tap_count)
    ]
    return dict(
        row_index=row_index,
        column_index=column_index,
        shifts=shifts,
        strict=jnp.where(same & (row_index > column_index), 1.0, 0.0),
        within=jnp.where(same & (row_index >= column_index), 1.0, 0.0),
        upto=jnp.where(row_index >= column_index, 1.0, 0.0),
        later=jnp.where(row_index > column_index, 1.0, 0.0),
        inside=inside,
    )


def conv_head(signal, taps, shifts):
    total = taps[-1] * signal
    for offset, shift in enumerate(shifts, 1):
        total = total + taps[len(taps) - 1 - offset] * fp_dot(shift, signal, 1, 0)
    return total * lax.logistic(total)


def unit_rows(values):
    return values * lax.rsqrt(jnp.sum(values * values, axis=1, keepdims=True) + epsilon)


def mixer_head(masks, inverse, bias, linears, taps, rate, norm_gain):
    query_lin, key_lin, value_lin, gate_lin, decay_lin, rate_lin = linears
    differentiated = inverse is not None
    queries = unit_rows(conv_head(query_lin, taps[0], masks["shifts"]))
    queries = queries * queries.shape[1] ** (-0.5)
    keys = unit_rows(conv_head(key_lin, taps[1], masks["shifts"]))
    values = conv_head(value_lin, taps[2], masks["shifts"])
    write_rate = lax.logistic(rate_lin)
    ramp = smooth_ramp if differentiated else plain_softplus
    log_decay = -rate * ramp(decay_lin + bias)
    ratio = jnp.exp(fp_dot(masks["upto"], log_decay * masks["later"], 1, 0))
    lower_part = write_rate * ratio * fp_dot(keys, keys, 1, 1) * masks["strict"]
    target = write_rate * values
    if differentiated:
        writes = apply_inverse(inverse, lower_part, target)
    else:
        inverse = unit_lower_inverse(lower_part, masks["row_index"], masks["column_index"])
        writes = fp_dot(inverse, target, 1, 0)
    heads = fp_dot(ratio * fp_dot(queries, keys, 1, 1) * masks["within"], writes, 1, 0)
    mean_square = jnp.sum(heads * heads, axis=1, keepdims=True) * (1.0 / heads.shape[1])
    normed = heads * lax.rsqrt(mean_square + epsilon) * norm_gain
    gated = normed * (gate_lin * lax.logistic(gate_lin)) * masks["inside"]
    return (gated, inverse)


LANES = 128
MESH = pl.DeviceIdType.MESH


def head_operands(h, heads, lin_ref, conv_refs, log_ref, bias_ref, gain_ref):
    length = lin_ref.shape[0]
    key_size = conv_refs[0].shape[1] // heads
    value_size = conv_refs[2].shape[1] // heads
    widths = (key_size, key_size, value_size, value_size)
    spans = []
    base = 0
    for width in widths:
        spans.append(slice(base + h * width, base + (h + 1) * width))
        base += heads * width
    tail = lin_ref[:, base : base + LANES]
    lane = lax.broadcasted_iota(jnp.int32, tail.shape, 1)
    columns = [
        jnp.sum(jnp.where(lane == place, tail, 0.0), axis=1, keepdims=True)
        for place in (h, heads + h)
    ]
    linears = tuple(lin_ref[:, span] for span in spans) + tuple(columns)
    tap_spans = [slice(h * width, (h + 1) * width) for width in widths[:3]]
    taps = tuple(
        tuple(ref[i : i + 1, span] for i in range(ref.shape[0]))
        for ref, span in zip(conv_refs, tap_spans)
    )
    rate = jnp.exp(jnp.full((length, 1), log_ref[h], jnp.float32))
    bias = jnp.full((length, 1), bias_ref[h], jnp.float32)
    return linears, taps, rate, bias, gain_ref[...], spans, tap_spans, base


def spread_columns(columns):
    shape = (columns[0].shape[0], LANES)
    lane = lax.broadcasted_iota(jnp.int32, shape, 1)
    total = jnp.zeros(shape, jnp.float32)
    for place, column in enumerate(columns):
        total = total + jnp.where(lane == place, column, 0.0)
    return total


def wrap(index, count):
    return lax.rem(index, count)


def dot_nn(left, right):
    return lax.dot_general(
        left, right, (((1,), (0,)), ((), ())), preferred_element_type=jnp.float32
    )


def dot_nt(left, right):
    return lax.dot_general(
        left, right, (((1,), (1,)), ((), ())), preferred_element_type=jnp.float32
    )


def dot_tn(left, right):
    return lax.dot_general(
        left, right, (((0,), (0,)), ((), ())), preferred_element_type=jnp.float32
    )


def diagonal(length):
    row = lax.broadcasted_iota(jnp.int32, (length, length), 0)
    column = lax.broadcasted_iota(jnp.int32, (length, length), 1)
    return row == column


def as_row(column):
    length = column.shape[0]
    return jnp.sum(jnp.where(diagonal(length), column, 0.0), axis=0, keepdims=True)


def as_column(row):
    length = row.shape[1]
    return jnp.sum(jnp.where(diagonal(length), row, 0.0), axis=1, keepdims=True)


class Link:
    def __init__(self, axis, count, me, landing, sems, place):
        self.axis, self.count, self.me = axis, count, me
        self.landing, self.sems, self.place = landing, sems, place
        self.source = None

    def copy(self, source, target, slot):
        return pltpu.make_async_remote_copy(
            src_ref=source,
            dst_ref=self.landing.at[slot],
            send_sem=self.sems.at[self.place, 0, target],
            recv_sem=self.sems.at[self.place, 1, slot],
            device_id={self.axis: target},
            device_id_type=MESH,
        )

    def send(self, source, target):
        self.copy(source, target, self.me).start()

    def spread(self):
        source = self.landing.at[self.me]
        for k in range(1, self.count):
            self.send(source, wrap(self.me + k, self.count))

    def arrive(self, slot):
        self.copy(self.landing.at[slot], slot, slot).wait_recv()

    def drain(self):
        for k in range(1, self.count):
            target = wrap(self.me + k, self.count)
            source = self.landing.at[self.me] if self.source is None else self.source.at[target]
            self.copy(source, target, self.me).wait_send()


def block_kernel(sizes, names, *flat):
    ref = types.SimpleNamespace(**dict(zip(names, flat)))
    groups, rows, cols, heads, features = sizes
    d, r, c = lax.axis_index("dp"), lax.axis_index("row"), lax.axis_index("col")
    sems, far_sems, dp_sems = ref.sems, ref.far_sems, ref.dp_sems
    grid_sems, half_sems = ref.grid_sems, ref.half_sems
    spread_count = groups * cols
    mine = d * cols + c

    barrier = pltpu.get_barrier_semaphore()
    for k in range(1, rows):
        pl.semaphore_signal(
            barrier, inc=1, device_id={"row": wrap(r + k, rows)}, device_id_type=MESH
        )

    def greet(k, carry):
        other = wrap(mine + k, spread_count)
        pl.semaphore_signal(
            barrier,
            inc=1,
            device_id={"dp": other // cols, "col": wrap(other, cols)},
            device_id_type=MESH,
        )
        return carry

    lax.fori_loop(1, spread_count, greet, 0)
    pl.semaphore_wait(barrier, rows - 1 + spread_count - 1)

    links = []

    def link_row(landing):
        links.append(Link("row", rows, r, landing, sems, len(links)))
        return links[-1]

    def link_col(landing):
        links.append(Link("col", cols, c, landing, sems, len(links)))
        return links[-1]

    x_link, og_link = link_col(ref.xng), link_row(ref.og4.at[c])
    b_link, ss1_link = link_row(ref.xr), link_row(ref.ss1_recv)
    mix_link, d_link = link_row(ref.mixg), link_col(ref.d_recv)
    n2_link, ss2_link = link_row(ref.n24.at[c]), link_row(ref.ss2_recv)
    wg_links = [link_row(ref.ffn_sum.at[half]) for half in ((d,) if groups == 2 else (0, 1))]
    i_link, o_link = link_row(ref.i_recv), link_row(ref.o_recv)
    t2c_link, t2_link = link_col(ref.t2c_recv), link_row(ref.t2g)
    gr_link, k_link = link_col(ref.grg), link_row(ref.k_recv)
    l_links = [link_row(ref.lg.at[h]) for h in range(heads)]
    lt_link, t1_link = link_row(ref.lt), link_row(ref.t1g)
    m_link, t1c_link = link_col(ref.m_recv), link_col(ref.t1_recv)
    p_link = link_row(ref.p_recv)

    def grid_copy(place, source, landing, target, slot, j):
        return pltpu.make_async_remote_copy(
            src_ref=source,
            dst_ref=landing.at[slot, j],
            send_sem=grid_sems.at[place, 0, target, j],
            recv_sem=grid_sems.at[place, 1, slot, j],
            device_id={"col": target},
            device_id_type=MESH,
        )

    halves = (d,) if groups == 2 else (0, 1)
    half_sent = []

    def half_copy(place, hop, source, landing, target, slot, half, peer):
        return pltpu.make_async_remote_copy(
            src_ref=source,
            dst_ref=landing.at[slot, half],
            send_sem=half_sems.at[place, hop, 0, target, half],
            recv_sem=half_sems.at[place, hop, 1, slot, half],
            device_id=peer,
            device_id_type=MESH,
        )

    def weights_out(place, source, landing):
        for k in range(1, rows):
            t = wrap(r + k, rows)
            for half in halves:
                copy = half_copy(place, 0, source(t, half), landing, t, r, half, {"row": t})
                copy.start()
                half_sent.append(copy)

    def weights_across(place, landing):
        for k in range(1, rows):
            j = wrap(r + k, rows)
            for half in halves:
                here = landing.at[j, half]
                half_copy(place, 0, here, landing, j, j, half, {"row": j}).wait_recv()
                if groups == 2:
                    copy = half_copy(place, 1, here, landing, j, j, half, {"dp": 1 - d})
                    copy.start()
                    half_sent.append(copy)

    def weights_in(place, landing):
        if groups == 2:
            for k in range(1, rows):
                j = wrap(r + k, rows)
                here = landing.at[j, 1 - d]
                half_copy(place, 1, here, landing, j, j, 1 - d, {"dp": 1 - d}).wait_recv()

    grid_sent = []

    def grid_send(place, source, landing, target, j):
        copy = grid_copy(place, source, landing, target, c, j)
        copy.start()
        grid_sent.append(copy)

    def grid_arrive(place, landing, slot, j):
        grid_copy(place, landing.at[slot, j], landing, slot, slot, j).wait_recv()

    def onward(row_link, place, blocks):
        for k in range(rows):
            j = gathered(row_link, k)
            for step in range(1, cols):
                grid_send(place, blocks.at[c, j], blocks, wrap(c + step, cols), j)

    def gathered(link_used, k):
        slot = wrap(link_used.me + k, link_used.count)
        if k:
            link_used.arrive(slot)
        return slot

    def pass_on(link_used, send, target):
        link_used.source = send

        @pl.when(target != link_used.me)
        def _():
            link_used.send(send.at[target], target)

    def total(link_used, send):
        running = send[link_used.me].astype(jnp.float32)
        for k in range(1, link_used.count):
            slot = wrap(link_used.me + k, link_used.count)
            link_used.arrive(slot)
            running = running + link_used.landing[slot].astype(jnp.float32)
        return running

    bf16 = jnp.bfloat16

    ref.og4[c, r] = ref.out_grad[...]

    def send_squares(link_used, values):
        sums = link_used.landing
        sums[r, 0:1, :] = as_row(jnp.sum(values * values, axis=1, keepdims=True))
        link_used.spread()

    def row_scale(link_used):
        sums = link_used.landing
        for k in range(1, rows):
            link_used.arrive(wrap(r + k, rows))
        running = sums[0, 0:1, :]
        for j in range(1, rows):
            running = running + sums[j, 0:1, :]
        return lax.rsqrt(as_column(running) * (1.0 / features) + epsilon)

    gain1 = ref.gain1[...]
    gain2 = ref.gain2[...]
    inputs = ref.x[...].astype(jnp.float32)
    send_squares(ss1_link, inputs)
    narrow = [source[...].astype(jnp.float32) for source in (ref.wd, ref.wb)]
    rows_of = [block[i : i + 1, :] for block in narrow for i in range(heads)]
    ref.wt[...] = spread_columns([as_column(row) for row in rows_of]).astype(bf16)
    in_refs = (ref.wq, ref.wk, ref.wv, ref.wg, ref.wt)
    in_spans = []
    base = 0
    depth = ref.w_all.shape[2]
    for weight in in_refs:
        width = weight.shape[1]
        in_spans.append(slice(base, base + width))
        base += width
        for half in range(2):
            ref.w_all[r, half, :, in_spans[-1]] = weight[half * depth : (half + 1) * depth, :]
    scale1 = row_scale(ss1_link)
    weights_out(0, lambda t, half: ref.w_all.at[r, half], ref.w_all)
    ref.xng[c] = (inputs * scale1 * gain1).astype(bf16)
    x_link.spread()
    for k in range(cols):
        t = gathered(x_link, k)
        pass_on(b_link, ref.xng, t)
    og_link.spread()

    hidden, width = ref.down.shape
    part = hidden // rows
    for place, weight in enumerate((ref.gate, ref.up, ref.down)):
        for j in range(rows):
            for half in range(2):
                ref.ffn_send[j, half, place * part : (place + 1) * part, :] = weight[
                    j * part : (j + 1) * part, half * depth : (half + 1) * depth
                ]
    weights_out(1, lambda t, half: ref.ffn_send.at[t, half], ref.ffn_all)
    ref.ffn_all[r] = ref.ffn_send[r]

    def share(j, span):
        return jnp.concatenate([ref.ffn_all[j, half, span, :] for half in range(2)], axis=1)


    def row_total(link_used, send):
        running = send[link_used.me, 0:1, :]
        for k in range(1, link_used.count):
            slot = wrap(link_used.me + k, link_used.count)
            link_used.arrive(slot)
            running = running + link_used.landing[slot, 0:1, :]
        return running

    ref.xr[r] = ref.xng[r]
    weights_across(0, ref.w_all)
    for k in range(1, rows):
        b_link.arrive(wrap(r + k, rows))
    weights_in(0, ref.w_all)
    for span in in_spans:
        ref.lin[:, span] = sum(
            dot_nn(ref.xr[j], ref.w_all[j, :, :, span].reshape(2 * depth, span.stop - span.start))
            for j in range(rows)
        )
    lin_ref = ref.lin
    length = lin_ref.shape[0]
    conv_refs = (ref.qc, ref.kc, ref.vc)
    slot_index = d * cols + r
    starts = [ref.starts[i, slot_index] for i in range(ref.starts.shape[0])]
    counts = [ref.counts[i, slot_index] for i in range(ref.counts.shape[0])]
    masks = slot_masks((starts, counts), length, conv_refs[0].shape[0])
    for h in range(heads):
        linears, taps, rate, bias, gain, _, tap_spans, _ = head_operands(
            h, heads, lin_ref, conv_refs, ref.log, ref.bias, ref.norm_gain
        )
        gated, inverse = mixer_head(masks, None, bias, linears, taps, rate, gain)
        ref.mixg[r, :, tap_spans[2]] = gated.astype(bf16)
        ref.inverse[h] = inverse
    mix_link.spread()
    for k in range(rows):
        t = gathered(mix_link, k)
        ref.d_send[t] = dot_nn(ref.mixg[t], ref.wo[...])
        pass_on(d_link, ref.d_send, t)
    onward(og_link, 0, ref.og4)
    weights_across(1, ref.ffn_all)
    resid = inputs + total(d_link, ref.d_send)
    ref.resid[...] = resid
    send_squares(ss2_link, resid)
    scale2 = row_scale(ss2_link)
    ref.n24[c, r] = (resid * scale2 * gain2).astype(bf16)
    n2_link.spread()
    onward(n2_link, 1, ref.n24)

    weights_in(1, ref.ffn_all)
    token = lax.broadcasted_iota(jnp.int32, (length, 1), 0)
    places = [slice(i * part, (i + 1) * part) for i in range(3)]
    for k in range(cols):
        t = wrap(c + k, cols)
        if k:
            for j in range(rows):
                grid_arrive(0, ref.og4, t, j)
            for j in range(rows):
                grid_arrive(1, ref.n24, t, j)
        gate_part, up_part, grad_hidden = (
            sum(dot_nt(tokens[t, j], share(j, span)) for j in range(rows))
            for tokens, span in zip((ref.n24, ref.n24, ref.og4), places)
        )
        inside = jnp.zeros((length, 1), jnp.float32)
        for i in range(ref.starts.shape[0]):
            begin = ref.starts[i, d * cols + t]
            end = begin + ref.counts[i, d * cols + t]
            inside += jnp.where((token >= begin) & (token < end), 1.0, 0.0)
        grad_hidden = grad_hidden * inside
        sigmoid = lax.logistic(gate_part)
        ref.hid[t] = (gate_part * sigmoid * up_part * inside).astype(bf16)
        grad_gate = grad_hidden * up_part * sigmoid * (1.0 + gate_part * (1.0 - sigmoid))
        grad_up = grad_hidden * gate_part * sigmoid
        ref.gg[t] = grad_gate.astype(bf16)
        ref.gu[t] = grad_up.astype(bf16)
        inner_sum = jnp.sum(grad_gate * gate_part + grad_up * up_part, axis=1, keepdims=True)
        ref.t2_send[t, 0:1, :] = as_row(inner_sum)
        pass_on(t2c_link, ref.t2_send, t)

    def all_tokens(source):
        block = source[...]
        return block.reshape(block.shape[0] * block.shape[1], block.shape[2])

    def feature_sums(place, send, landing, grads):
        for k in range(1, rows + 1):
            j = wrap(r + k, rows)
            terms = sum(dot_nn(grad, share(j, span)) for grad, span in grads)
            for t in range(cols):
                send[t, j] = terms[t * length : (t + 1) * length].astype(bf16)
            for step in range(1, cols):
                t = wrap(c + step, cols)
                grid_send(place, send.at[t, j], landing, t, j)

    def across_rows(place, send, landing, row_link, row_send):
        for k in range(1, rows + 1):
            j = wrap(r + k, rows)
            running = send[c, j].astype(jnp.float32)
            for step in range(1, cols):
                t = wrap(c + step, cols)
                grid_arrive(place, landing, t, j)
                running = running + landing[t, j].astype(jnp.float32)
            row_send[j] = running.astype(bf16)
            pass_on(row_link, row_send, j)

    feature_sums(
        2, ref.gi_send, ref.gi_recv,
        ((all_tokens(ref.gg), places[0]), (all_tokens(ref.gu), places[1])),
    )
    ref.t2g[r, 0:1, :] = row_total(t2c_link, ref.t2_send)
    t2_link.spread()
    across_rows(2, ref.gi_send, ref.gi_recv, i_link, ref.i_send)

    dp_copies = []

    def trade(source, landing, part):
        if groups == 2:
            copy = pltpu.make_async_remote_copy(
                src_ref=source,
                dst_ref=landing,
                send_sem=dp_sems.at[part, 0],
                recv_sem=dp_sems.at[part, 1],
                device_id={"dp": 1 - d},
                device_id_type=MESH,
            )
            copy.start()
            dp_copies.append(copy)
            return copy

    grad_second = total(i_link, ref.i_send) * scale2
    t2 = as_column(row_total(t2_link, ref.t2g)) * scale2 * scale2 * (1.0 / features)
    resid = ref.resid[...]
    grad_resid = ref.out_grad[...].astype(jnp.float32) + grad_second * gain2 - resid * t2
    ref.grad_resid[...] = grad_resid
    ref.grg[c] = grad_resid.astype(bf16)
    gr_link.spread()
    ffn_gain_part = jnp.sum(grad_second * resid, axis=0, keepdims=True)

    for k in range(cols):
        t = gathered(gr_link, k)
        ref.k_send[t] = dot_nt(ref.grg[t], ref.wo[...]).astype(bf16)
        pass_on(k_link, ref.k_send, t)
    sides = ((ref.gg, ref.n24), (ref.gu, ref.n24), (ref.hid, ref.og4))
    lefts = [all_tokens(left) for left, _ in sides]
    for j in range(rows):
        for span, left, (_, right) in zip(places, lefts, sides):
            tokens = right[:, j].reshape(cols * length, width)
            grads = dot_tn(left, tokens).astype(bf16)
            for half in range(2):
                ref.wg_send[half, j, span, :] = grads[:, half * depth : (half + 1) * depth]
    if groups == 2:
        wg_trade = trade(ref.wg_send.at[1 - d], ref.wg_recv, 1)
    feature_sums(3, ref.go_send, ref.go_recv, ((all_tokens(ref.hid), places[2]),))
    ref.pair_out[0] = dot_tn(all_tokens(ref.mixg), all_tokens(ref.grg)).astype(bf16)
    trade(ref.pair_out.at[0], ref.pair_out.at[1], 0)
    across_rows(3, ref.go_send, ref.go_recv, o_link, ref.o_send)

    ref.upstream[...] = total(k_link, ref.k_send)
    if groups == 2:
        wg_trade.wait_recv()
        dp_copies.remove(wg_trade)
        for k in range(1, rows + 1):
            j = wrap(r + k, rows)
            both = ref.wg_send[d, j].astype(jnp.float32) + ref.wg_recv[j].astype(jnp.float32)
            ref.wg_sum[j] = both.astype(bf16)
            pass_on(wg_links[0], ref.wg_sum, j)
        ref.ffn_sum[d, r] = ref.wg_sum[r]
    else:
        for half in range(2):
            for k in range(1, rows):
                pass_on(wg_links[half], ref.wg_send.at[half], wrap(r + k, rows))
            ref.ffn_sum[half, r] = ref.wg_send[half, r]
    masks = slot_masks((starts, counts), length, conv_refs[0].shape[0])
    decay_columns, rate_columns, log_columns = [], [], []
    gain_total = jnp.zeros(ref.norm_gain.shape, jnp.float32)
    inner_sum = jnp.zeros((length, 1), jnp.float32)
    params = ref.p_recv
    params[r] = jnp.zeros(params.shape[1:], jnp.float32)
    taps_count = conv_refs[0].shape[0]
    key_width = conv_refs[0].shape[1]
    head_spans, head_weights = [], [[] for h in range(heads)]
    base = 0
    for weight in in_refs[:4]:
        size = weight.shape[1] // heads
        head_spans.append(slice(base, base + size))
        base += size
        for h in range(heads):
            head_weights[h].append((weight, slice(h * size, (h + 1) * size)))
    for h in range(heads):
        linears, taps, rate, bias, gain, spans, tap_spans, tail_base = head_operands(
            h, heads, lin_ref, conv_refs, ref.log, ref.bias, ref.norm_gain
        )
        inverse = ref.inverse[h]

        def piece(linear_set, tap_set, rate_set, gain_set):
            return mixer_head(masks, inverse, bias, linear_set, tap_set, rate_set, gain_set)[0]

        _, back = jax.vjp(piece, linears, taps, rate, gain)
        grad_linears, grad_taps, grad_rate, grad_gain = back(ref.upstream[:, tap_spans[2]])
        for span, grad in zip(head_spans, grad_linears):
            ref.lg[h, r, :, span] = grad.astype(bf16)
        if h + 1 < heads:
            l_links[h].spread()
        for grad, linear in zip(grad_linears, linears):
            inner_sum = inner_sum + jnp.sum(grad * linear, axis=1, keepdims=True)
        places = ((taps_count, 0), (taps_count, key_width), (0, 0))
        for (top, left), span, grads in zip(places, tap_spans, grad_taps):
            for i, grad in enumerate(grads):
                params[r, top + i : top + i + 1, left + span.start : left + span.stop] = grad
        gain_total = gain_total + grad_gain
        decay_columns.append(grad_linears[4])
        rate_columns.append(grad_linears[5])
        log_columns.append(grad_rate * rate)
    tails = spread_columns(decay_columns + rate_columns)
    ref.lt[r] = tails.astype(bf16)
    lt_link.spread()
    ref.t1g[r, 0:1, :] = as_row(inner_sum)
    t1_link.spread()
    value_size = gain_total.shape[1]
    params[r, 2 * taps_count : 2 * taps_count + 1, 0:value_size] = gain_total
    params[r, 2 * taps_count + 1 : 2 * taps_count + 2, 0:LANES] = jnp.sum(
        spread_columns(log_columns + decay_columns), axis=0, keepdims=True
    )
    p_link.spread()
    l_links[heads - 1].spread()
    ref.output[...] = (ref.resid[...] + total(o_link, ref.o_send)).astype(bf16)
    for used in wg_links:
        for k in range(1, rows):
            used.arrive(wrap(r + k, rows))
    trade(ref.ffn_sum.at[d], ref.ffn_sum.at[d], 2)

    first_all = all_tokens(ref.xng)

    def head_grads(h):
        ref.pair_in[0, h] = dot_tn(first_all, all_tokens(ref.lg.at[h])).astype(bf16)
        trade(ref.pair_in.at[0, h], ref.pair_in.at[1, h], 4 + h)

    for h in range(heads - 1):
        for k in range(rows):
            gathered(l_links[h], k)
        head_grads(h)
    for k in range(rows):
        t = gathered(t1_link, k)
        pass_on(t1c_link, ref.t1g, t)
        gathered(lt_link, k)
        gathered(l_links[heads - 1], k)
        terms = dot_nt(ref.lt[t], ref.wt[...])
        for h in range(heads):
            for span, (weight, columns) in zip(head_spans, head_weights[h]):
                terms = terms + dot_nt(ref.lg[h, t, :, span], weight[:, columns])
        ref.m_send[t] = terms.astype(bf16)
        pass_on(m_link, ref.m_send, t)
    ref.pair_tail[0] = dot_tn(first_all, all_tokens(ref.lt)).astype(bf16)
    trade(ref.pair_tail.at[0], ref.pair_tail.at[1], 3)
    head_grads(heads - 1)

    for k in range(1, rows):
        p_link.arrive(wrap(r + k, rows))
    summed = params[0]
    for j in range(1, rows):
        summed = summed + params[j]
    far_p, far_g = ref.far_p, ref.far_g
    far_p[d] = summed

    def far_copy(landing, place, slot, target, peer):
        return pltpu.make_async_remote_copy(
            src_ref=landing.at[slot],
            dst_ref=landing.at[slot],
            send_sem=far_sems.at[place, 0, target],
            recv_sem=far_sems.at[place, 1, slot],
            device_id=peer,
            device_id_type=MESH,
        )

    def dp_peers(act):
        def step(k, carry):
            other = wrap(d + k, groups)
            act(other, {"dp": other})
            return carry

        lax.fori_loop(1, groups, step, 0)

    def far_peers(act):
        def step(k, carry):
            other = wrap(mine + k, spread_count)
            act(other, {"dp": other // cols, "col": wrap(other, cols)})
            return carry

        lax.fori_loop(1, spread_count, step, 0)

    dp_peers(lambda other, peer: far_copy(far_p, 0, d, other, peer).start())

    grad_first = total(m_link, ref.m_send) * scale1
    t1 = as_column(row_total(t1c_link, ref.t1g)) * scale1 * scale1 * (1.0 / features)
    ref.input_grad[...] = ref.grad_resid[...] + grad_first * gain1 - inputs * t1
    far_g[mine] = jnp.zeros(far_g.shape[1:], jnp.float32)
    far_g[mine, 0:1, :] = jnp.sum(grad_first * inputs, axis=0, keepdims=True)
    far_g[mine, 1:2, :] = ffn_gain_part
    far_g[mine, 2:3, 0:value_size] = summed[2 * taps_count : 2 * taps_count + 1, 0:value_size]
    far_peers(lambda other, peer: far_copy(far_g, 1, mine, other, peer).start())
    dp_peers(lambda other, peer: far_copy(far_p, 0, other, other, peer).wait_recv())
    far_peers(lambda other, peer: far_copy(far_g, 1, other, other, peer).wait_recv())
    ref.params[...] = lax.fori_loop(1, groups, lambda j, acc: acc + far_p[j], far_p[0])
    ref.gains[...] = lax.fori_loop(1, spread_count, lambda j, acc: acc + far_g[j], far_g[0])
    for copy in dp_copies:
        copy.wait_recv()

    dp_peers(lambda other, peer: far_copy(far_p, 0, d, other, peer).wait_send())
    far_peers(lambda other, peer: far_copy(far_g, 1, mine, other, peer).wait_send())
    for copy in dp_copies:
        copy.wait_send()
    if groups == 2:
        wg_trade.wait_send()
    for copy in grid_sent + half_sent:
        copy.wait_send()
    for used in links:
        used.drain()


def finish_kernel(heads, taps_count, *refs):
    (pair_in, pair_tail, pair_out, ffn_sum, params, gains, out_in, grad_in) = refs[:8]
    (output, input_grad, attn, gq, gk, gv, gg, gd, gb, cq, ck, cv, dl, db, hg, go, fg, gate, up, down) = refs[8:]

    def both(pair, *index):
        return pair[(0,) + index].astype(jnp.float32) + pair[(1,) + index].astype(jnp.float32)

    output[...] = out_in[...]
    input_grad[...] = grad_in[...]
    attn[...] = gains[0:1, :]
    fg[...] = gains[1:2, :]
    hg[...] = gains[2:3, 0 : hg.shape[1]]
    base = 0
    every = slice(None)
    for ref in (gq, gk, gv, gg):
        size = ref.shape[1] // heads
        for h in range(heads):
            ref[:, h * size : (h + 1) * size] = both(pair_in, h, every, slice(base, base + size))
        base += size
    tail = both(pair_tail)
    for i in range(heads):
        lane = lax.broadcasted_iota(jnp.int32, tail.shape, 1)
        for ref, place in ((gd, i), (gb, heads + i)):
            column = jnp.sum(jnp.where(lane == place, tail, 0.0), axis=1, keepdims=True)
            ref[i : i + 1, :] = as_row(column)
    key_width = cq.shape[1]
    cv[...] = params[0:taps_count, :]
    cq[...] = params[taps_count : 2 * taps_count, 0:key_width]
    ck[...] = params[taps_count : 2 * taps_count, key_width : 2 * key_width]
    dl[...] = params[2 * taps_count + 1 : 2 * taps_count + 2, 0:heads]
    db[...] = params[2 * taps_count + 1 : 2 * taps_count + 2, heads : 2 * heads]
    go[...] = both(pair_out)
    rows, part = ffn_sum.shape[1], ffn_sum.shape[2] // 3
    def units(j, place):
        span = slice(place * part, (place + 1) * part)
        return jnp.concatenate([ffn_sum[half, j, span, :] for half in range(2)], axis=1)

    for place, ref in enumerate((gate, up, down)):
        for j in range(rows):
            ref[j * part : (j + 1) * part, :] = units(j, place).astype(jnp.float32)


def shards(
    block_input,
    attn_gain,
    query_weight,
    key_weight,
    value_weight,
    gate_weight,
    decay_weight,
    beta_weight,
    query_conv,
    key_conv,
    value_conv,
    decay_log,
    decay_bias,
    head_gain,
    out_weight,
    ffn_gain,
    ffn_gate,
    ffn_up,
    ffn_down,
    out_grad,
    seq_starts,
    seq_lengths,
):
    groups, rows, cols = (lax.axis_size(name) for name in ("dp", "row", "col"))
    length, width = block_input.shape
    heads = decay_log.shape[0]
    taps_count = query_conv.shape[0]
    keys, values = query_weight.shape[1], value_weight.shape[1]
    hidden = ffn_gate.shape[1]
    part = hidden // rows
    in_width = 2 * keys + 2 * values + LANES
    head_width = 2 * (keys + values) // heads
    bf16, f32 = jnp.bfloat16, jnp.float32
    smem = pl.BlockSpec(memory_space=pltpu.SMEM)
    vmem = pl.BlockSpec(memory_space=pltpu.VMEM)
    operands = dict(
        starts=seq_starts.T, counts=seq_lengths.T, log=decay_log, bias=decay_bias,
        x=block_input, gain1=attn_gain[None, :], wq=query_weight, wk=key_weight,
        wv=value_weight, wg=gate_weight, wd=decay_weight.T, wb=beta_weight.T, qc=query_conv, kc=key_conv,
        vc=value_conv, norm_gain=head_gain[None, :], wo=out_weight, gain2=ffn_gain[None, :],
        gate=ffn_gate.T, up=ffn_up.T, down=ffn_down, out_grad=out_grad,
    )
    param_shape = (2 * taps_count + 8, max(2 * keys, values))
    gains_shape = (8, max(width, head_gain.shape[0]))
    results = dict(
        output=((length, width), bf16),
        input_grad=((length, width), f32),
        pair_in=((2, heads, width, head_width), bf16),
        pair_tail=((2, width, LANES), bf16),
        pair_out=((2, values, width), bf16),
        ffn_sum=((2, rows, 3 * part, width // 2), bf16),
        params=(param_shape, f32),
        gains=(gains_shape, f32),
    )
    token_block = (cols, length, width)
    vector = (8, length)
    side_block = (rows, 3 * part, width // 2)
    half_block = ((rows, 2, 3 * part, width // 2), bf16)
    grid_block = ((cols, rows, length, width), bf16)
    row_block = ((rows, length, width), bf16)
    unit_block = ((cols, length, part), bf16)
    scratch = dict(
        wt=((width, LANES), bf16), xng=(token_block, bf16), og4=grid_block, n24=grid_block,
        xr=((rows, length, width), bf16), w_all=((rows, 2, width // 2, in_width), bf16),
        ss1_recv=((rows,) + vector, f32), ss2_recv=((rows,) + vector, f32),
        lin=((length, in_width), f32), inverse=((heads, length, length), f32),
        mixg=((rows, length, values), bf16),
        d_send=(token_block, f32), d_recv=(token_block, f32),
        resid=((length, width), f32),
        ffn_send=half_block, ffn_all=half_block,
        wg_send=((2,) + side_block, bf16), wg_recv=(side_block, bf16), wg_sum=(side_block, bf16),
        hid=unit_block, gg=unit_block, gu=unit_block,
        t2_send=((cols,) + vector, f32), t2c_recv=((cols,) + vector, f32),
        t2g=((rows,) + vector, f32),
        gi_send=grid_block, gi_recv=grid_block, i_send=row_block, i_recv=row_block,
        go_send=grid_block, go_recv=grid_block, o_send=row_block, o_recv=row_block,
        grad_resid=((length, width), f32), grg=(token_block, bf16),
        k_send=((rows, length, values), bf16), k_recv=((rows, length, values), bf16),
        upstream=((length, values), f32),
        lg=((heads, rows, length, head_width), bf16), lt=((rows, length, LANES), bf16), t1g=((rows,) + vector, f32),
        m_send=(token_block, bf16), m_recv=(token_block, bf16), t1_recv=((cols,) + vector, f32),
        p_recv=((rows,) + param_shape, f32),
        far_p=((groups,) + param_shape, f32),
        far_g=((groups * cols,) + gains_shape, f32),
    )
    link_count = 20 + heads + 1
    semaphores = dict(
        sems=pltpu.SemaphoreType.DMA((link_count, 2, max(rows, cols))),
        far_sems=pltpu.SemaphoreType.DMA((2, 2, groups * cols)),
        dp_sems=pltpu.SemaphoreType.DMA((4 + heads, 2)),
        half_sems=pltpu.SemaphoreType.DMA((2, 2, 2, rows, 2)),
        grid_sems=pltpu.SemaphoreType.DMA((4, 2, cols, rows)),
    )
    names = tuple(operands) + tuple(results) + tuple(scratch) + tuple(semaphores)
    features = width * rows
    made = pl.pallas_call(
        functools.partial(block_kernel, (groups, rows, cols, heads, features), names),
        out_shape=tuple(jax.ShapeDtypeStruct(*entry) for entry in results.values()),
        in_specs=[smem] * 4 + [vmem] * (len(operands) - 4),
        out_specs=tuple([vmem] * len(results)),
        scratch_shapes=[pltpu.VMEM(*entry) for entry in scratch.values()]
        + list(semaphores.values()),
        compiler_params=pltpu.CompilerParams(
            collective_id=0, has_side_effects=True, vmem_limit_bytes=58 * 1024 * 1024
        ),
        name="residual_block",
    )(*operands.values())
    made = list(made)
    if groups != 2:
        for place in range(2, 5):
            whole = lax.psum(made[place][0], "dp")
            made[place] = jnp.stack([whole, jnp.zeros_like(whole)])
        made[5] = lax.psum(made[5], "dp")
    finals = (
        block_input, jax.ShapeDtypeStruct((length, width), f32), attn_gain[None, :],
        query_weight, key_weight, value_weight, gate_weight, decay_weight.T, beta_weight.T,
        query_conv, key_conv, value_conv, decay_log[None, :], decay_bias[None, :],
        head_gain[None, :], out_weight, ffn_gain[None, :], ffn_gate.T, ffn_up.T, ffn_down,
    )
    given = made[2:] + made[:2]
    final = pl.pallas_call(
        functools.partial(finish_kernel, heads, taps_count),
        out_shape=tuple(
            jax.ShapeDtypeStruct(entry.shape, bf16 if place == 0 else f32)
            for place, entry in enumerate(finals)
        ),
        in_specs=[vmem] * len(given),
        out_specs=tuple([vmem] * len(finals)),
        compiler_params=pltpu.CompilerParams(vmem_limit_bytes=58 * 1024 * 1024),
        name="group_sums",
    )(*given)
    final = list(final)
    for place in (2, 12, 13, 14, 16):
        final[place] = final[place][0]
    for place in (7, 8, 17, 18):
        final[place] = final[place].T
    return tuple(final)


def solution(mesh):
    in_specs = (
        P(("dp", "col"), "row"),
        P("row"),
        P("row", "col"),
        P("row", "col"),
        P("row", "col"),
        P("row", "col"),
        P("row", "col"),
        P("row", "col"),
        P(None, "col"),
        P(None, "col"),
        P(None, "col"),
        P("col"),
        P("col"),
        P(),
        P("col", "row"),
        P("row"),
        P("row", "col"),
        P("row", "col"),
        P("col", "row"),
        P(("dp", "col"), "row"),
        P(),
        P(),
    )
    out_specs = (
        P(("dp", "col"), "row"),
        P(("dp", "col"), "row"),
        P("row"),
        P("row", "col"),
        P("row", "col"),
        P("row", "col"),
        P("row", "col"),
        P("row", "col"),
        P("row", "col"),
        P(None, "col"),
        P(None, "col"),
        P(None, "col"),
        P("col"),
        P("col"),
        P(),
        P("col", "row"),
        P("row"),
        P("row", "col"),
        P("row", "col"),
        P("col", "row"),
    )
    return jax.shard_map(shards, mesh=mesh, in_specs=in_specs, out_specs=out_specs, check_vma=False)
```

```python
import functools
import types

import jax
import jax.numpy as jnp
from jax import lax
from jax.experimental import pallas as pl
from jax.experimental.pallas import tpu as pltpu
from jax.sharding import PartitionSpec as P

epsilon = 1e-06
highest = lax.Precision.HIGHEST


def fp_dot(left, right, left_dim, right_dim):
    return lax.dot_general(
        left,
        right,
        (((left_dim,), (right_dim,)), ((), ())),
        precision=highest,
        preferred_element_type=jnp.float32,
    )


def plain_softplus(values):
    return jnp.maximum(values, 0.0) + jnp.log1p(jnp.exp(-jnp.abs(values)))


@jax.custom_vjp
def smooth_ramp(values):
    return plain_softplus(values)


smooth_ramp.defvjp(
    lambda values: (plain_softplus(values), values),
    lambda values, upstream: (upstream * lax.logistic(values),),
)


@jax.custom_vjp
def apply_inverse(inverse, lower_part, target):
    return fp_dot(inverse, target, 1, 0)


def apply_inverse_forward(inverse, lower_part, target):
    writes = fp_dot(inverse, target, 1, 0)
    return writes, (inverse, writes)


def apply_inverse_backward(saved, upstream):
    inverse, writes = saved
    grad_target = fp_dot(inverse, upstream, 0, 0)
    return (jnp.zeros_like(inverse), -fp_dot(grad_target, writes, 1, 1), grad_target)


apply_inverse.defvjp(apply_inverse_forward, apply_inverse_backward)


def unit_lower_inverse(lower_part, row_index, column_index):
    length = lower_part.shape[0]
    inverse = jnp.where(row_index == column_index, 1.0, 0.0)
    level = 0
    while (1 << level) < length:
        row_block = row_index >> level
        column_block = column_index >> level
        joined = (row_block == column_block + 1) & ((column_block & 1) == 0)
        corner = jnp.where(joined, lower_part, 0.0)
        if level == 0:
            inverse = inverse - corner
        else:
            inverse = inverse - fp_dot(fp_dot(inverse, corner, 1, 0), inverse, 1, 0)
        level += 1
    return inverse


def slot_masks(bounds, length, tap_count):
    row_index = lax.broadcasted_iota(jnp.int32, (length, length), 0)
    column_index = lax.broadcasted_iota(jnp.int32, (length, length), 1)
    token = lax.broadcasted_iota(jnp.int32, (length, 1), 0)
    row_segment = jnp.zeros((length, length), jnp.int32)
    column_segment = jnp.zeros((length, length), jnp.int32)
    inside = jnp.zeros((length, 1), jnp.float32)
    for begin, count in zip(*bounds):
        end = begin + count
        row_segment += jnp.where(row_index >= begin, 1, 0) + jnp.where(row_index >= end, 1, 0)
        column_segment += jnp.where(column_index >= begin, 1, 0)
        column_segment += jnp.where(column_index >= end, 1, 0)
        inside += jnp.where((token >= begin) & (token < end), 1.0, 0.0)
    same = row_segment == column_segment
    shifts = [
        jnp.where(same & (column_index == row_index - offset), 1.0, 0.0)
        for offset in range(1, tap_count)
    ]
    return dict(
        row_index=row_index,
        column_index=column_index,
        shifts=shifts,
        strict=jnp.where(same & (row_index > column_index), 1.0, 0.0),
        within=jnp.where(same & (row_index >= column_index), 1.0, 0.0),
        upto=jnp.where(row_index >= column_index, 1.0, 0.0),
        later=jnp.where(row_index > column_index, 1.0, 0.0),
        inside=inside,
    )


def conv_head(signal, taps, shifts):
    total = taps[-1] * signal
    for offset, shift in enumerate(shifts, 1):
        total = total + taps[len(taps) - 1 - offset] * fp_dot(shift, signal, 1, 0)
    return total * lax.logistic(total)


def unit_rows(values):
    return values * lax.rsqrt(jnp.sum(values * values, axis=1, keepdims=True) + epsilon)


def mixer_head(masks, inverse, bias, linears, taps, rate, norm_gain):
    query_lin, key_lin, value_lin, gate_lin, decay_lin, rate_lin = linears
    differentiated = inverse is not None
    queries = unit_rows(conv_head(query_lin, taps[0], masks["shifts"]))
    queries = queries * queries.shape[1] ** (-0.5)
    keys = unit_rows(conv_head(key_lin, taps[1], masks["shifts"]))
    values = conv_head(value_lin, taps[2], masks["shifts"])
    write_rate = lax.logistic(rate_lin)
    ramp = smooth_ramp if differentiated else plain_softplus
    log_decay = -rate * ramp(decay_lin + bias)
    ratio = jnp.exp(fp_dot(masks["upto"], log_decay * masks["later"], 1, 0))
    lower_part = write_rate * ratio * fp_dot(keys, keys, 1, 1) * masks["strict"]
    target = write_rate * values
    if differentiated:
        writes = apply_inverse(inverse, lower_part, target)
    else:
        inverse = unit_lower_inverse(lower_part, masks["row_index"], masks["column_index"])
        writes = fp_dot(inverse, target, 1, 0)
    heads = fp_dot(ratio * fp_dot(queries, keys, 1, 1) * masks["within"], writes, 1, 0)
    mean_square = jnp.sum(heads * heads, axis=1, keepdims=True) * (1.0 / heads.shape[1])
    normed = heads * lax.rsqrt(mean_square + epsilon) * norm_gain
    gated = normed * (gate_lin * lax.logistic(gate_lin)) * masks["inside"]
    return (gated, inverse)


LANES = 128
MESH = pl.DeviceIdType.MESH


def head_operands(h, heads, lin_ref, conv_refs, log_ref, bias_ref, gain_ref):
    length = lin_ref.shape[0]
    key_size = conv_refs[0].shape[1] // heads
    value_size = conv_refs[2].shape[1] // heads
    widths = (key_size, key_size, value_size, value_size)
    spans = []
    base = 0
    for width in widths:
        spans.append(slice(base + h * width, base + (h + 1) * width))
        base += heads * width
    tail = lin_ref[:, base : base + LANES]
    lane = lax.broadcasted_iota(jnp.int32, tail.shape, 1)
    columns = [
        jnp.sum(jnp.where(lane == place, tail, 0.0), axis=1, keepdims=True)
        for place in (h, heads + h)
    ]
    linears = tuple(lin_ref[:, span] for span in spans) + tuple(columns)
    tap_spans = [slice(h * width, (h + 1) * width) for width in widths[:3]]
    taps = tuple(
        tuple(ref[i : i + 1, span] for i in range(ref.shape[0]))
        for ref, span in zip(conv_refs, tap_spans)
    )
    rate = jnp.exp(jnp.full((length, 1), log_ref[h], jnp.float32))
    bias = jnp.full((length, 1), bias_ref[h], jnp.float32)
    return linears, taps, rate, bias, gain_ref[...], spans, tap_spans, base


def spread_columns(columns):
    shape = (columns[0].shape[0], LANES)
    lane = lax.broadcasted_iota(jnp.int32, shape, 1)
    total = jnp.zeros(shape, jnp.float32)
    for place, column in enumerate(columns):
        total = total + jnp.where(lane == place, column, 0.0)
    return total


def wrap(index, count):
    return lax.rem(index, count)


def dot_nn(left, right):
    return lax.dot_general(
        left, right, (((1,), (0,)), ((), ())), preferred_element_type=jnp.float32
    )


def dot_nt(left, right):
    return lax.dot_general(
        left, right, (((1,), (1,)), ((), ())), preferred_element_type=jnp.float32
    )


def dot_tn(left, right):
    return lax.dot_general(
        left, right, (((0,), (0,)), ((), ())), preferred_element_type=jnp.float32
    )


def diagonal(length):
    row = lax.broadcasted_iota(jnp.int32, (length, length), 0)
    column = lax.broadcasted_iota(jnp.int32, (length, length), 1)
    return row == column


def as_row(column):
    length = column.shape[0]
    return jnp.sum(jnp.where(diagonal(length), column, 0.0), axis=0, keepdims=True)


def as_column(row):
    length = row.shape[1]
    return jnp.sum(jnp.where(diagonal(length), row, 0.0), axis=1, keepdims=True)


class Link:
    def __init__(self, axis, count, me, landing, sems, place):
        self.axis, self.count, self.me = axis, count, me
        self.landing, self.sems, self.place = landing, sems, place
        self.source = None

    def copy(self, source, target, slot):
        return pltpu.make_async_remote_copy(
            src_ref=source,
            dst_ref=self.landing.at[slot],
            send_sem=self.sems.at[self.place, 0, target],
            recv_sem=self.sems.at[self.place, 1, slot],
            device_id={self.axis: target},
            device_id_type=MESH,
        )

    def send(self, source, target):
        self.copy(source, target, self.me).start()

    def spread(self):
        source = self.landing.at[self.me]
        for k in range(1, self.count):
            self.send(source, wrap(self.me + k, self.count))

    def arrive(self, slot):
        self.copy(self.landing.at[slot], slot, slot).wait_recv()

    def drain(self):
        for k in range(1, self.count):
            target = wrap(self.me + k, self.count)
            source = self.landing.at[self.me] if self.source is None else self.source.at[target]
            self.copy(source, target, self.me).wait_send()


def block_kernel(sizes, names, *flat):
    ref = types.SimpleNamespace(**dict(zip(names, flat)))
    groups, rows, cols, heads, features = sizes
    d, r, c = lax.axis_index("dp"), lax.axis_index("row"), lax.axis_index("col")
    sems, far_sems, dp_sems = ref.sems, ref.far_sems, ref.dp_sems
    grid_sems, half_sems = ref.grid_sems, ref.half_sems
    spread_count = groups * cols
    mine = d * cols + c

    barrier = pltpu.get_barrier_semaphore()
    for k in range(1, rows):
        pl.semaphore_signal(
            barrier, inc=1, device_id={"row": wrap(r + k, rows)}, device_id_type=MESH
        )

    def greet(k, carry):
        other = wrap(mine + k, spread_count)
        pl.semaphore_signal(
            barrier,
            inc=1,
            device_id={"dp": other // cols, "col": wrap(other, cols)},
            device_id_type=MESH,
        )
        return carry

    lax.fori_loop(1, spread_count, greet, 0)
    pl.semaphore_wait(barrier, rows - 1 + spread_count - 1)

    links = []

    def link_row(landing):
        links.append(Link("row", rows, r, landing, sems, len(links)))
        return links[-1]

    def link_col(landing):
        links.append(Link("col", cols, c, landing, sems, len(links)))
        return links[-1]

    x_link, og_link = link_col(ref.xng), link_row(ref.og4.at[c])
    b_link, ss1_link = link_row(ref.xr), link_row(ref.ss1_recv)
    mix_links = [link_row(ref.mixg.at[h]) for h in range(heads)]
    d_link = link_col(ref.d_recv)
    n2_link, ss2_link = link_row(ref.n24.at[c]), link_row(ref.ss2_recv)
    wg_links = [link_row(ref.ffn_sum.at[half]) for half in ((d,) if groups == 2 else (0, 1))]
    i_link, o_link = link_row(ref.i_recv), link_row(ref.o_recv)
    t2c_link, t2_link = link_col(ref.t2c_recv), link_row(ref.t2g)
    gr_link = link_col(ref.grg)
    k_links = [link_row(ref.k_recv.at[h]) for h in range(heads)]
    l_links = [link_row(ref.lg.at[h]) for h in range(heads)]
    lt_link, t1_link = link_row(ref.lt), link_row(ref.t1g)
    m_link, t1c_link = link_col(ref.m_recv), link_col(ref.t1_recv)
    p_link = link_row(ref.p_recv)

    def grid_copy(place, source, landing, target, slot, j):
        return pltpu.make_async_remote_copy(
            src_ref=source,
            dst_ref=landing.at[slot, j],
            send_sem=grid_sems.at[place, 0, target, j],
            recv_sem=grid_sems.at[place, 1, slot, j],
            device_id={"col": target},
            device_id_type=MESH,
        )

    halves = (d,) if groups == 2 else (0, 1)
    half_sent = []

    def half_copy(place, hop, source, landing, target, slot, half, peer):
        return pltpu.make_async_remote_copy(
            src_ref=source,
            dst_ref=landing.at[slot, half],
            send_sem=half_sems.at[place, hop, 0, target, half],
            recv_sem=half_sems.at[place, hop, 1, slot, half],
            device_id=peer,
            device_id_type=MESH,
        )

    def weights_out(place, source, landing):
        for k in range(1, rows):
            t = wrap(r + k, rows)
            for half in halves:
                copy = half_copy(place, 0, source(t, half), landing, t, r, half, {"row": t})
                copy.start()
                half_sent.append(copy)

    def weights_across(place, landing):
        for k in range(1, rows):
            j = wrap(r + k, rows)
            for half in halves:
                here = landing.at[j, half]
                half_copy(place, 0, here, landing, j, j, half, {"row": j}).wait_recv()
                if groups == 2:
                    copy = half_copy(place, 1, here, landing, j, j, half, {"dp": 1 - d})
                    copy.start()
                    half_sent.append(copy)

    def weights_in(place, landing):
        if groups == 2:
            for k in range(1, rows):
                j = wrap(r + k, rows)
                here = landing.at[j, 1 - d]
                half_copy(place, 1, here, landing, j, j, 1 - d, {"dp": 1 - d}).wait_recv()

    grid_sent = []

    def grid_send(place, source, landing, target, j):
        copy = grid_copy(place, source, landing, target, c, j)
        copy.start()
        grid_sent.append(copy)

    def grid_arrive(place, landing, slot, j):
        grid_copy(place, landing.at[slot, j], landing, slot, slot, j).wait_recv()

    paired = cols % 2 == 0

    def beside(slot):
        return slot + 1 - 2 * wrap(slot, 2)

    def onward_paired(row_link, place, blocks):
        for k in range(rows):
            j = gathered(row_link, k)
            for step in range(2, cols, 2):
                grid_send(place, blocks.at[c, j], blocks, wrap(c + step, cols), j)
            grid_send(place, blocks.at[c, j], blocks, beside(c), j)
        for k in range(rows):
            j = wrap(r + k, rows)
            for step in range(2, cols, 2):
                t = wrap(c + step, cols)
                grid_arrive(place, blocks, t, j)
                copy = pltpu.make_async_remote_copy(
                    src_ref=blocks.at[t, j],
                    dst_ref=blocks.at[t, j],
                    send_sem=grid_sems.at[place, 0, beside(t), j],
                    recv_sem=grid_sems.at[place, 1, t, j],
                    device_id={"col": beside(c)},
                    device_id_type=MESH,
                )
                copy.start()
                grid_sent.append(copy)

    def onward(row_link, place, blocks):
        for k in range(rows):
            j = gathered(row_link, k)
            for step in range(1, cols):
                grid_send(place, blocks.at[c, j], blocks, wrap(c + step, cols), j)

    def gathered(link_used, k):
        slot = wrap(link_used.me + k, link_used.count)
        if k:
            link_used.arrive(slot)
        return slot

    def pass_on(link_used, send, target):
        link_used.source = send

        @pl.when(target != link_used.me)
        def _():
            link_used.send(send.at[target], target)

    def total(link_used, send):
        running = send[link_used.me].astype(jnp.float32)
        for k in range(1, link_used.count):
            slot = wrap(link_used.me + k, link_used.count)
            link_used.arrive(slot)
            running = running + link_used.landing[slot].astype(jnp.float32)
        return running

    bf16 = jnp.bfloat16

    ref.og4[c, r] = ref.out_grad[...]

    def send_squares(link_used, values):
        sums = link_used.landing
        sums[r, 0:1, :] = as_row(jnp.sum(values * values, axis=1, keepdims=True))
        link_used.spread()

    def row_scale(link_used):
        sums = link_used.landing
        for k in range(1, rows):
            link_used.arrive(wrap(r + k, rows))
        running = sums[0, 0:1, :]
        for j in range(1, rows):
            running = running + sums[j, 0:1, :]
        return lax.rsqrt(as_column(running) * (1.0 / features) + epsilon)

    gain1 = ref.gain1[...]
    gain2 = ref.gain2[...]
    inputs = ref.x[...].astype(jnp.float32)
    send_squares(ss1_link, inputs)
    narrow = [source[...].astype(jnp.float32) for source in (ref.wd, ref.wb)]
    rows_of = [block[i : i + 1, :] for block in narrow for i in range(heads)]
    ref.wt[...] = spread_columns([as_column(row) for row in rows_of]).astype(bf16)
    in_refs = (ref.wq, ref.wk, ref.wv, ref.wg, ref.wt)
    in_spans = []
    base = 0
    depth = ref.w_all.shape[2]
    for weight in in_refs:
        width = weight.shape[1]
        in_spans.append(slice(base, base + width))
        base += width
        for half in range(2):
            ref.w_all[r, half, :, in_spans[-1]] = weight[half * depth : (half + 1) * depth, :]
    scale1 = row_scale(ss1_link)
    weights_out(0, lambda t, half: ref.w_all.at[r, half], ref.w_all)
    ref.xng[c] = (inputs * scale1 * gain1).astype(bf16)
    x_link.spread()
    for k in range(cols):
        t = gathered(x_link, k)
        pass_on(b_link, ref.xng, t)
    og_link.spread()

    hidden, width = ref.down.shape
    part = hidden // rows
    for place, weight in enumerate((ref.gate, ref.up, ref.down)):
        for j in range(rows):
            for half in range(2):
                ref.ffn_send[j, half, place * part : (place + 1) * part, :] = weight[
                    j * part : (j + 1) * part, half * depth : (half + 1) * depth
                ]
    weights_out(1, lambda t, half: ref.ffn_send.at[t, half], ref.ffn_all)
    ref.ffn_all[r] = ref.ffn_send[r]

    def share(j, span):
        return jnp.concatenate([ref.ffn_all[j, half, span, :] for half in range(2)], axis=1)


    def row_total(link_used, send):
        running = send[link_used.me, 0:1, :]
        for k in range(1, link_used.count):
            slot = wrap(link_used.me + k, link_used.count)
            link_used.arrive(slot)
            running = running + link_used.landing[slot, 0:1, :]
        return running

    ref.xr[r] = ref.xng[r]
    weights_across(0, ref.w_all)
    for k in range(1, rows):
        b_link.arrive(wrap(r + k, rows))
    weights_in(0, ref.w_all)
    for span in in_spans:
        ref.lin[:, span] = sum(
            dot_nn(ref.xr[j], ref.w_all[j, :, :, span].reshape(2 * depth, span.stop - span.start))
            for j in range(rows)
        )
    lin_ref = ref.lin
    length = lin_ref.shape[0]
    conv_refs = (ref.qc, ref.kc, ref.vc)
    slot_index = d * cols + r
    starts = [ref.starts[i, slot_index] for i in range(ref.starts.shape[0])]
    counts = [ref.counts[i, slot_index] for i in range(ref.counts.shape[0])]
    masks = slot_masks((starts, counts), length, conv_refs[0].shape[0])
    for h in range(heads):
        linears, taps, rate, bias, gain, _, tap_spans, _ = head_operands(
            h, heads, lin_ref, conv_refs, ref.log, ref.bias, ref.norm_gain
        )
        gated, inverse = mixer_head(masks, None, bias, linears, taps, rate, gain)
        ref.mixg[h, r] = gated.astype(bf16)
        mix_links[h].spread()
        ref.inverse[h] = inverse
    value_size = ref.norm_gain.shape[1]
    head_rows = [slice(h * value_size, (h + 1) * value_size) for h in range(heads)]
    for k in range(rows):
        for used in mix_links:
            t = gathered(used, k)
        ref.d_send[t] = sum(dot_nn(ref.mixg[h, t], ref.wo[head_rows[h], :]) for h in range(heads))
        pass_on(d_link, ref.d_send, t)
    onward(og_link, 0, ref.og4)
    weights_across(1, ref.ffn_all)
    resid = inputs + total(d_link, ref.d_send)
    ref.resid[...] = resid
    send_squares(ss2_link, resid)
    scale2 = row_scale(ss2_link)
    ref.n24[c, r] = (resid * scale2 * gain2).astype(bf16)
    n2_link.spread()
    if paired:
        onward_paired(n2_link, 1, ref.n24)
    else:
        onward(n2_link, 1, ref.n24)

    weights_in(1, ref.ffn_all)
    token = lax.broadcasted_iota(jnp.int32, (length, 1), 0)
    places = [slice(i * part, (i + 1) * part) for i in range(3)]
    for k in range(cols):
        t = wrap(c + k, cols)
        if k:
            for j in range(rows):
                grid_arrive(0, ref.og4, t, j)
            if k % 2 or not paired:
                for j in range(rows):
                    grid_arrive(1, ref.n24, t, j)
        gate_part, up_part, grad_hidden = (
            sum(dot_nt(tokens[t, j], share(j, span)) for j in range(rows))
            for tokens, span in zip((ref.n24, ref.n24, ref.og4), places)
        )
        inside = jnp.zeros((length, 1), jnp.float32)
        for i in range(ref.starts.shape[0]):
            begin = ref.starts[i, d * cols + t]
            end = begin + ref.counts[i, d * cols + t]
            inside += jnp.where((token >= begin) & (token < end), 1.0, 0.0)
        grad_hidden = grad_hidden * inside
        sigmoid = lax.logistic(gate_part)
        ref.hid[t] = (gate_part * sigmoid * up_part * inside).astype(bf16)
        grad_gate = grad_hidden * up_part * sigmoid * (1.0 + gate_part * (1.0 - sigmoid))
        grad_up = grad_hidden * gate_part * sigmoid
        ref.gg[t] = grad_gate.astype(bf16)
        ref.gu[t] = grad_up.astype(bf16)
        inner_sum = jnp.sum(grad_gate * gate_part + grad_up * up_part, axis=1, keepdims=True)
        ref.t2_send[t, 0:1, :] = as_row(inner_sum)
        pass_on(t2c_link, ref.t2_send, t)

    def all_tokens(source):
        block = source[...]
        return block.reshape(block.shape[0] * block.shape[1], block.shape[2])

    def feature_sums(place, send, landing, grads):
        for k in range(1, rows + 1):
            j = wrap(r + k, rows)
            terms = sum(dot_nn(grad, share(j, span)) for grad, span in grads)
            for t in range(cols):
                send[t, j] = terms[t * length : (t + 1) * length].astype(bf16)
            for step in range(1, cols):
                t = wrap(c + step, cols)
                grid_send(place, send.at[t, j], landing, t, j)

    def across_rows(place, send, landing, row_link, row_send):
        for k in range(1, rows + 1):
            j = wrap(r + k, rows)
            running = send[c, j].astype(jnp.float32)
            for step in range(1, cols):
                t = wrap(c + step, cols)
                grid_arrive(place, landing, t, j)
                running = running + landing[t, j].astype(jnp.float32)
            row_send[j] = running.astype(bf16)
            pass_on(row_link, row_send, j)

    feature_sums(
        2, ref.gi_send, ref.gi_recv,
        ((all_tokens(ref.gg), places[0]), (all_tokens(ref.gu), places[1])),
    )
    ref.t2g[r, 0:1, :] = row_total(t2c_link, ref.t2_send)
    t2_link.spread()
    across_rows(2, ref.gi_send, ref.gi_recv, i_link, ref.i_send)

    dp_copies = []

    def trade(source, landing, part):
        if groups == 2:
            copy = pltpu.make_async_remote_copy(
                src_ref=source,
                dst_ref=landing,
                send_sem=dp_sems.at[part, 0],
                recv_sem=dp_sems.at[part, 1],
                device_id={"dp": 1 - d},
                device_id_type=MESH,
            )
            copy.start()
            dp_copies.append(copy)
            return copy

    grad_second = total(i_link, ref.i_send) * scale2
    t2 = as_column(row_total(t2_link, ref.t2g)) * scale2 * scale2 * (1.0 / features)
    resid = ref.resid[...]
    grad_resid = ref.out_grad[...].astype(jnp.float32) + grad_second * gain2 - resid * t2
    ref.grad_resid[...] = grad_resid
    ref.grg[c] = grad_resid.astype(bf16)
    gr_link.spread()
    ffn_gain_part = jnp.sum(grad_second * resid, axis=0, keepdims=True)

    for h in range(heads):
        for k in range(cols):
            t = gathered(gr_link, k) if h == 0 else wrap(c + k, cols)
            ref.k_send[h, t] = dot_nt(ref.grg[t], ref.wo[head_rows[h], :]).astype(bf16)
            pass_on(k_links[h], ref.k_send.at[h], t)
    sides = ((ref.gg, ref.n24), (ref.gu, ref.n24), (ref.hid, ref.og4))
    lefts = [all_tokens(left) for left, _ in sides]
    for j in range(rows):
        for span, left, (_, right) in zip(places, lefts, sides):
            tokens = right[:, j].reshape(cols * length, width)
            grads = dot_tn(left, tokens).astype(bf16)
            for half in range(2):
                ref.wg_send[half, j, span, :] = grads[:, half * depth : (half + 1) * depth]
    if groups == 2:
        wg_trade = trade(ref.wg_send.at[1 - d], ref.wg_recv, 1)
    feature_sums(3, ref.go_send, ref.go_recv, ((all_tokens(ref.hid), places[2]),))
    for h in range(heads):
        ref.pair_out[0, head_rows[h], :] = dot_tn(
            all_tokens(ref.mixg.at[h]), all_tokens(ref.grg)
        ).astype(bf16)
    trade(ref.pair_out.at[0], ref.pair_out.at[1], 0)
    across_rows(3, ref.go_send, ref.go_recv, o_link, ref.o_send)

    ref.upstream[:, head_rows[0]] = total(k_links[0], ref.k_send.at[0])
    if groups == 2:
        wg_trade.wait_recv()
        dp_copies.remove(wg_trade)
        for k in range(1, rows + 1):
            j = wrap(r + k, rows)
            both = ref.wg_send[d, j].astype(jnp.float32) + ref.wg_recv[j].astype(jnp.float32)
            ref.wg_sum[j] = both.astype(bf16)
            pass_on(wg_links[0], ref.wg_sum, j)
        ref.ffn_sum[d, r] = ref.wg_sum[r]
    else:
        for half in range(2):
            for k in range(1, rows):
                pass_on(wg_links[half], ref.wg_send.at[half], wrap(r + k, rows))
            ref.ffn_sum[half, r] = ref.wg_send[half, r]
    masks = slot_masks((starts, counts), length, conv_refs[0].shape[0])
    decay_columns, rate_columns, log_columns = [], [], []
    gain_total = jnp.zeros(ref.norm_gain.shape, jnp.float32)
    inner_sum = jnp.zeros((length, 1), jnp.float32)
    params = ref.p_recv
    params[r] = jnp.zeros(params.shape[1:], jnp.float32)
    taps_count = conv_refs[0].shape[0]
    key_width = conv_refs[0].shape[1]
    head_spans, head_weights = [], [[] for h in range(heads)]
    base = 0
    for weight in in_refs[:4]:
        size = weight.shape[1] // heads
        head_spans.append(slice(base, base + size))
        base += size
        for h in range(heads):
            head_weights[h].append((weight, slice(h * size, (h + 1) * size)))
    for h in range(heads):
        linears, taps, rate, bias, gain, spans, tap_spans, tail_base = head_operands(
            h, heads, lin_ref, conv_refs, ref.log, ref.bias, ref.norm_gain
        )
        inverse = ref.inverse[h]
        if h:
            ref.upstream[:, head_rows[h]] = total(k_links[h], ref.k_send.at[h])

        def piece(linear_set, tap_set, rate_set, gain_set):
            return mixer_head(masks, inverse, bias, linear_set, tap_set, rate_set, gain_set)[0]

        _, back = jax.vjp(piece, linears, taps, rate, gain)
        grad_linears, grad_taps, grad_rate, grad_gain = back(ref.upstream[:, tap_spans[2]])
        for span, grad in zip(head_spans, grad_linears):
            ref.lg[h, r, :, span] = grad.astype(bf16)
        if h + 1 < heads:
            l_links[h].spread()
        for grad, linear in zip(grad_linears, linears):
            inner_sum = inner_sum + jnp.sum(grad * linear, axis=1, keepdims=True)
        places = ((taps_count, 0), (taps_count, key_width), (0, 0))
        for (top, left), span, grads in zip(places, tap_spans, grad_taps):
            for i, grad in enumerate(grads):
                params[r, top + i : top + i + 1, left + span.start : left + span.stop] = grad
        gain_total = gain_total + grad_gain
        decay_columns.append(grad_linears[4])
        rate_columns.append(grad_linears[5])
        log_columns.append(grad_rate * rate)
    tails = spread_columns(decay_columns + rate_columns)
    ref.lt[r] = tails.astype(bf16)
    lt_link.spread()
    ref.t1g[r, 0:1, :] = as_row(inner_sum)
    t1_link.spread()
    value_size = gain_total.shape[1]
    params[r, 2 * taps_count : 2 * taps_count + 1, 0:value_size] = gain_total
    params[r, 2 * taps_count + 1 : 2 * taps_count + 2, 0:LANES] = jnp.sum(
        spread_columns(log_columns + decay_columns), axis=0, keepdims=True
    )
    p_link.spread()
    l_links[heads - 1].spread()
    ref.output[...] = (ref.resid[...] + total(o_link, ref.o_send)).astype(bf16)
    for used in wg_links:
        for k in range(1, rows):
            used.arrive(wrap(r + k, rows))
    trade(ref.ffn_sum.at[d], ref.ffn_sum.at[d], 2)

    first_all = all_tokens(ref.xng)

    def head_grads(h):
        ref.pair_in[0, h] = dot_tn(first_all, all_tokens(ref.lg.at[h])).astype(bf16)
        trade(ref.pair_in.at[0, h], ref.pair_in.at[1, h], 4 + h)

    for h in range(heads - 1):
        for k in range(rows):
            gathered(l_links[h], k)
        head_grads(h)
    for k in range(rows):
        t = gathered(t1_link, k)
        pass_on(t1c_link, ref.t1g, t)
        gathered(lt_link, k)
        gathered(l_links[heads - 1], k)
        terms = dot_nt(ref.lt[t], ref.wt[...])
        for h in range(heads):
            for span, (weight, columns) in zip(head_spans, head_weights[h]):
                terms = terms + dot_nt(ref.lg[h, t, :, span], weight[:, columns])
        ref.m_send[t] = terms.astype(bf16)
        pass_on(m_link, ref.m_send, t)
    ref.pair_tail[0] = dot_tn(first_all, all_tokens(ref.lt)).astype(bf16)
    trade(ref.pair_tail.at[0], ref.pair_tail.at[1], 3)
    head_grads(heads - 1)

    for k in range(1, rows):
        p_link.arrive(wrap(r + k, rows))
    summed = params[0]
    for j in range(1, rows):
        summed = summed + params[j]
    far_p, far_g = ref.far_p, ref.far_g
    far_p[d] = summed

    def far_copy(landing, place, slot, target, peer):
        return pltpu.make_async_remote_copy(
            src_ref=landing.at[slot],
            dst_ref=landing.at[slot],
            send_sem=far_sems.at[place, 0, target],
            recv_sem=far_sems.at[place, 1, slot],
            device_id=peer,
            device_id_type=MESH,
        )

    def dp_peers(act):
        def step(k, carry):
            other = wrap(d + k, groups)
            act(other, {"dp": other})
            return carry

        lax.fori_loop(1, groups, step, 0)

    def far_peers(act):
        def step(k, carry):
            other = wrap(mine + k, spread_count)
            act(other, {"dp": other // cols, "col": wrap(other, cols)})
            return carry

        lax.fori_loop(1, spread_count, step, 0)

    dp_peers(lambda other, peer: far_copy(far_p, 0, d, other, peer).start())

    grad_first = total(m_link, ref.m_send) * scale1
    t1 = as_column(row_total(t1c_link, ref.t1g)) * scale1 * scale1 * (1.0 / features)
    ref.input_grad[...] = ref.grad_resid[...] + grad_first * gain1 - inputs * t1
    far_g[mine] = jnp.zeros(far_g.shape[1:], jnp.float32)
    far_g[mine, 0:1, :] = jnp.sum(grad_first * inputs, axis=0, keepdims=True)
    far_g[mine, 1:2, :] = ffn_gain_part
    far_g[mine, 2:3, 0:value_size] = summed[2 * taps_count : 2 * taps_count + 1, 0:value_size]
    far_peers(lambda other, peer: far_copy(far_g, 1, mine, other, peer).start())
    dp_peers(lambda other, peer: far_copy(far_p, 0, other, other, peer).wait_recv())
    far_peers(lambda other, peer: far_copy(far_g, 1, other, other, peer).wait_recv())
    ref.params[...] = lax.fori_loop(1, groups, lambda j, acc: acc + far_p[j], far_p[0])
    ref.gains[...] = lax.fori_loop(1, spread_count, lambda j, acc: acc + far_g[j], far_g[0])
    for copy in dp_copies:
        copy.wait_recv()

    dp_peers(lambda other, peer: far_copy(far_p, 0, d, other, peer).wait_send())
    far_peers(lambda other, peer: far_copy(far_g, 1, mine, other, peer).wait_send())
    for copy in dp_copies:
        copy.wait_send()
    if groups == 2:
        wg_trade.wait_send()
    for copy in grid_sent + half_sent:
        copy.wait_send()
    for used in links:
        used.drain()


def finish_kernel(heads, taps_count, *refs):
    (pair_in, pair_tail, pair_out, ffn_sum, params, gains, out_in, grad_in) = refs[:8]
    (output, input_grad, attn, gq, gk, gv, gg, gd, gb, cq, ck, cv, dl, db, hg, go, fg, gate, up, down) = refs[8:]

    def both(pair, *index):
        return pair[(0,) + index].astype(jnp.float32) + pair[(1,) + index].astype(jnp.float32)

    output[...] = out_in[...]
    input_grad[...] = grad_in[...]
    attn[...] = gains[0:1, :]
    fg[...] = gains[1:2, :]
    hg[...] = gains[2:3, 0 : hg.shape[1]]
    base = 0
    every = slice(None)
    for ref in (gq, gk, gv, gg):
        size = ref.shape[1] // heads
        for h in range(heads):
            ref[:, h * size : (h + 1) * size] = both(pair_in, h, every, slice(base, base + size))
        base += size
    tail = both(pair_tail)
    for i in range(heads):
        lane = lax.broadcasted_iota(jnp.int32, tail.shape, 1)
        for ref, place in ((gd, i), (gb, heads + i)):
            column = jnp.sum(jnp.where(lane == place, tail, 0.0), axis=1, keepdims=True)
            ref[i : i + 1, :] = as_row(column)
    key_width = cq.shape[1]
    cv[...] = params[0:taps_count, :]
    cq[...] = params[taps_count : 2 * taps_count, 0:key_width]
    ck[...] = params[taps_count : 2 * taps_count, key_width : 2 * key_width]
    dl[...] = params[2 * taps_count + 1 : 2 * taps_count + 2, 0:heads]
    db[...] = params[2 * taps_count + 1 : 2 * taps_count + 2, heads : 2 * heads]
    go[...] = both(pair_out)
    rows, part = ffn_sum.shape[1], ffn_sum.shape[2] // 3
    def units(j, place):
        span = slice(place * part, (place + 1) * part)
        return jnp.concatenate([ffn_sum[half, j, span, :] for half in range(2)], axis=1)

    for place, ref in enumerate((gate, up, down)):
        for j in range(rows):
            ref[j * part : (j + 1) * part, :] = units(j, place).astype(jnp.float32)


def shards(
    block_input,
    attn_gain,
    query_weight,
    key_weight,
    value_weight,
    gate_weight,
    decay_weight,
    beta_weight,
    query_conv,
    key_conv,
    value_conv,
    decay_log,
    decay_bias,
    head_gain,
    out_weight,
    ffn_gain,
    ffn_gate,
    ffn_up,
    ffn_down,
    out_grad,
    seq_starts,
    seq_lengths,
):
    groups, rows, cols = (lax.axis_size(name) for name in ("dp", "row", "col"))
    length, width = block_input.shape
    heads = decay_log.shape[0]
    taps_count = query_conv.shape[0]
    keys, values = query_weight.shape[1], value_weight.shape[1]
    hidden = ffn_gate.shape[1]
    part = hidden // rows
    in_width = 2 * keys + 2 * values + LANES
    head_width = 2 * (keys + values) // heads
    bf16, f32 = jnp.bfloat16, jnp.float32
    smem = pl.BlockSpec(memory_space=pltpu.SMEM)
    vmem = pl.BlockSpec(memory_space=pltpu.VMEM)
    operands = dict(
        starts=seq_starts.T, counts=seq_lengths.T, log=decay_log, bias=decay_bias,
        x=block_input, gain1=attn_gain[None, :], wq=query_weight, wk=key_weight,
        wv=value_weight, wg=gate_weight, wd=decay_weight.T, wb=beta_weight.T, qc=query_conv, kc=key_conv,
        vc=value_conv, norm_gain=head_gain[None, :], wo=out_weight, gain2=ffn_gain[None, :],
        gate=ffn_gate.T, up=ffn_up.T, down=ffn_down, out_grad=out_grad,
    )
    param_shape = (2 * taps_count + 8, max(2 * keys, values))
    gains_shape = (8, max(width, head_gain.shape[0]))
    results = dict(
        output=((length, width), bf16),
        input_grad=((length, width), f32),
        pair_in=((2, heads, width, head_width), bf16),
        pair_tail=((2, width, LANES), bf16),
        pair_out=((2, values, width), bf16),
        ffn_sum=((2, rows, 3 * part, width // 2), bf16),
        params=(param_shape, f32),
        gains=(gains_shape, f32),
    )
    token_block = (cols, length, width)
    vector = (8, length)
    side_block = (rows, 3 * part, width // 2)
    half_block = ((rows, 2, 3 * part, width // 2), bf16)
    grid_block = ((cols, rows, length, width), bf16)
    row_block = ((rows, length, width), bf16)
    unit_block = ((cols, length, part), bf16)
    scratch = dict(
        wt=((width, LANES), bf16), xng=(token_block, bf16), og4=grid_block, n24=grid_block,
        xr=((rows, length, width), bf16), w_all=((rows, 2, width // 2, in_width), bf16),
        ss1_recv=((rows,) + vector, f32), ss2_recv=((rows,) + vector, f32),
        lin=((length, in_width), f32), inverse=((heads, length, length), f32),
        mixg=((heads, rows, length, values // heads), bf16),
        d_send=(token_block, f32), d_recv=(token_block, f32),
        resid=((length, width), f32),
        ffn_send=half_block, ffn_all=half_block,
        wg_send=((2,) + side_block, bf16), wg_recv=(side_block, bf16), wg_sum=(side_block, bf16),
        hid=unit_block, gg=unit_block, gu=unit_block,
        t2_send=((cols,) + vector, f32), t2c_recv=((cols,) + vector, f32),
        t2g=((rows,) + vector, f32),
        gi_send=grid_block, gi_recv=grid_block, i_send=row_block, i_recv=row_block,
        go_send=grid_block, go_recv=grid_block, o_send=row_block, o_recv=row_block,
        grad_resid=((length, width), f32), grg=(token_block, bf16),
        k_send=((heads, rows, length, values // heads), bf16),
        k_recv=((heads, rows, length, values // heads), bf16),
        upstream=((length, values), f32),
        lg=((heads, rows, length, head_width), bf16), lt=((rows, length, LANES), bf16), t1g=((rows,) + vector, f32),
        m_send=(token_block, bf16), m_recv=(token_block, bf16), t1_recv=((cols,) + vector, f32),
        p_recv=((rows,) + param_shape, f32),
        far_p=((groups,) + param_shape, f32),
        far_g=((groups * cols,) + gains_shape, f32),
    )
    link_count = 20 + 3 * heads + 1
    semaphores = dict(
        sems=pltpu.SemaphoreType.DMA((link_count, 2, max(rows, cols))),
        far_sems=pltpu.SemaphoreType.DMA((2, 2, groups * cols)),
        dp_sems=pltpu.SemaphoreType.DMA((4 + heads, 2)),
        half_sems=pltpu.SemaphoreType.DMA((2, 2, 2, rows, 2)),
        grid_sems=pltpu.SemaphoreType.DMA((4, 2, cols, rows)),
    )
    names = tuple(operands) + tuple(results) + tuple(scratch) + tuple(semaphores)
    features = width * rows
    made = pl.pallas_call(
        functools.partial(block_kernel, (groups, rows, cols, heads, features), names),
        out_shape=tuple(jax.ShapeDtypeStruct(*entry) for entry in results.values()),
        in_specs=[smem] * 4 + [vmem] * (len(operands) - 4),
        out_specs=tuple([vmem] * len(results)),
        scratch_shapes=[pltpu.VMEM(*entry) for entry in scratch.values()]
        + list(semaphores.values()),
        compiler_params=pltpu.CompilerParams(
            collective_id=0, has_side_effects=True, vmem_limit_bytes=58 * 1024 * 1024
        ),
        name="residual_block",
    )(*operands.values())
    made = list(made)
    if groups != 2:
        for place in range(2, 5):
            whole = lax.psum(made[place][0], "dp")
            made[place] = jnp.stack([whole, jnp.zeros_like(whole)])
        made[5] = lax.psum(made[5], "dp")
    finals = (
        block_input, jax.ShapeDtypeStruct((length, width), f32), attn_gain[None, :],
        query_weight, key_weight, value_weight, gate_weight, decay_weight.T, beta_weight.T,
        query_conv, key_conv, value_conv, decay_log[None, :], decay_bias[None, :],
        head_gain[None, :], out_weight, ffn_gain[None, :], ffn_gate.T, ffn_up.T, ffn_down,
    )
    given = made[2:] + made[:2]
    final = pl.pallas_call(
        functools.partial(finish_kernel, heads, taps_count),
        out_shape=tuple(
            jax.ShapeDtypeStruct(entry.shape, bf16 if place == 0 else f32)
            for place, entry in enumerate(finals)
        ),
        in_specs=[vmem] * len(given),
        out_specs=tuple([vmem] * len(finals)),
        compiler_params=pltpu.CompilerParams(vmem_limit_bytes=58 * 1024 * 1024),
        name="group_sums",
    )(*given)
    final = list(final)
    for place in (2, 12, 13, 14, 16):
        final[place] = final[place][0]
    for place in (7, 8, 17, 18):
        final[place] = final[place].T
    return tuple(final)


def solution(mesh):
    in_specs = (
        P(("dp", "col"), "row"),
        P("row"),
        P("row", "col"),
        P("row", "col"),
        P("row", "col"),
        P("row", "col"),
        P("row", "col"),
        P("row", "col"),
        P(None, "col"),
        P(None, "col"),
        P(None, "col"),
        P("col"),
        P("col"),
        P(),
        P("col", "row"),
        P("row"),
        P("row", "col"),
        P("row", "col"),
        P("col", "row"),
        P(("dp", "col"), "row"),
        P(),
        P(),
    )
    out_specs = (
        P(("dp", "col"), "row"),
        P(("dp", "col"), "row"),
        P("row"),
        P("row", "col"),
        P("row", "col"),
        P("row", "col"),
        P("row", "col"),
        P("row", "col"),
        P("row", "col"),
        P(None, "col"),
        P(None, "col"),
        P(None, "col"),
        P("col"),
        P("col"),
        P(),
        P("col", "row"),
        P("row"),
        P("row", "col"),
        P("row", "col"),
        P("col", "row"),
    )
    return jax.shard_map(shards, mesh=mesh, in_specs=in_specs, out_specs=out_specs, check_vma=False)
```
